128 devices in a mesh: mem: 4 (over z_lo, core), wide: 32 (over x, z_hi, y).
Axes of the slice: x: 4, y: 4, z: 4 (z_hi: 2, z_lo: 2; z = z_hi * 2 + z_lo), core: 2. Of those that a mesh axis runs over, the one named last changes fastest.
Arguments:
- control: float32 [8, 64, 128, 720], P('mem', 'wide'), may hold values from -6 to 6
- perturb: float32 [8, 3, 64, 128, 720], P('mem', None, None, 'wide'), may hold values from -6 to 6
- obs_count: int32 [128, 720], P('wide'), may hold values from 0 to 3
- obs_kind: int32 [128, 720], P('wide'), may hold values from 0 to 7
- obs_table: float32 [8, 192], replicated, may hold values from 0.25 to 4
- band_filter: float32 [64, 64], replicated, may hold values from -0.9 to 1.2, as said below
- diffusivity: float32 [128, 720], replicated, may hold values from 0.04 to 0.24
Outputs:
- hessian_product: float32 [8, 64, 128, 720], P('mem', 'wide')
The draws below stay inside these ranges and needn't reach their ends.
Inputs may be any that keep to these rules, and one draw needn't show every extreme that they name: band_filter[i, j] is zero where |i - j| > 4; its diagonal lies between 0.8 and 1.2.
All inputs are finite; a program needn't handle non-finite values.
Results may differ from the reference program's by a relative error of at most 0.00005.
Values sent between devices are 32-bit elements; how exact they have to be, the bound alone decides.
No kernel may reach another device: no remote copies, remote signals or barrier semaphores. Data moves between devices by JAX's collectives and lax.ppermute only.
A program may use at most 64 MiB of HBM per device.

```python
import math
import jax
import jax.numpy as jnp
from jax import lax

LEVELS = 64
NLAT = 128
NLON = 720
ITERS = 16
HB = 4
KINDS = 8
MEMBERS = 8


def draw_band_filter(key, part):
    row_index = lax.broadcasted_iota(jnp.int32, (LEVELS, LEVELS), 0)
    col_index = lax.broadcasted_iota(jnp.int32, (LEVELS, LEVELS), 1)
    in_band = jnp.abs(row_index - col_index) <= HB
    key_off = jax.random.fold_in(key, 11)
    key_diag = jax.random.fold_in(key, 23)
    off_band = jnp.clip(0.3 * jax.random.normal(key_off, (LEVELS, LEVELS), jnp.float32), -0.9, 0.9)
    diagonal = jax.random.uniform(key_diag, (LEVELS, LEVELS), jnp.float32, 0.8, 1.2)
    return jnp.where(row_index == col_index, diagonal, jnp.where(in_band, off_band, jnp.zeros_like(off_band)))


def with_ends(result, stream_key, low, top_value):
    place = [jax.random.randint(jax.random.fold_in(stream_key, axis), (), 0, length) for axis, length in enumerate(result.shape)]
    main_axis = result.shape.index(max(result.shape))
    neighbour = place[:main_axis] + [(place[main_axis] + 1) % result.shape[main_axis]] + place[main_axis + 1:]
    return result.at[tuple(place)].set(low).at[tuple(neighbour)].set(top_value)


def block_scale(own_key, extent, shards, least, largest):
    def one(axis_at, shards_of):
        steps = jax.random.uniform(jax.random.fold_in(jax.random.fold_in(own_key, 6), axis_at), (shards_of,), jnp.float32, least / len(shards), largest / len(shards))
        return jnp.repeat(jnp.exp(steps), extent[axis_at] // shards_of).reshape((-1,) + (1,) * (len(extent) - axis_at - 1))

    loudness = one(*shards[0])
    for cut in shards[1:]:
        loudness = loudness * one(*cut)
    return loudness


def normal_values(rng, shape, width, limit, split=(), dtype=jnp.bfloat16):
    level = block_scale(rng, shape, split, -0.22, 0.18) if split else 1.0
    values = jax.random.normal(rng, shape, jnp.float32) * width * level
    return jnp.minimum(jnp.maximum(values, -limit), limit).astype(dtype)


def setup_inputs(seed: int = 0) -> dict:
    keys = jax.random.split(jax.random.key(seed), 8)
    return {
        "control": normal_values(keys[0], (MEMBERS, LEVELS, NLAT, NLON), 1.0, 6.0, ((0, 4), (1, 32)), jnp.float32),
        "perturb": normal_values(keys[1], (MEMBERS, 3, LEVELS, NLAT, NLON), 1.0, 6.0, ((0, 4), (3, 32)), jnp.float32),
        "obs_count": with_ends(jax.random.randint(keys[2], (NLAT, NLON), 0, 4), jax.random.fold_in(keys[2], 1), 0, 3).astype(jnp.int32),
        "obs_kind": with_ends(jax.random.randint(keys[3], (NLAT, NLON), 0, KINDS), jax.random.fold_in(keys[3], 1), 0, KINDS - 1).astype(jnp.int32),
        "obs_table": jnp.clip(jnp.exp(jax.random.uniform(keys[4], (KINDS, 3 * LEVELS), jnp.float32, math.log(0.25), math.log(4.0))), 0.25, 4.0),
        "band_filter": draw_band_filter(jax.random.fold_in(keys[7], 71), 0),
        "diffusivity": jnp.clip(jax.random.uniform(keys[6], (NLAT, NLON), jnp.float32, 0.04, 0.24), 0.04, 0.24),
    }


def edge_coeffs(diffusivity):
    east_edge = 0.5 * (diffusivity + jnp.roll(diffusivity, -1, axis=1))
    north_edge = 0.5 * (diffusivity + jnp.roll(diffusivity, -1, axis=0))
    row_index = lax.broadcasted_iota(jnp.int32, diffusivity.shape, 0)
    north_edge = jnp.where(row_index < diffusivity.shape[0] - 1, north_edge, jnp.zeros_like(north_edge))
    return east_edge, north_edge


def diffuse(field, east_edge, north_edge):
    def one_step(step_index, field_now):
        flux_east = east_edge * (jnp.roll(field_now, -1, axis=-1) - field_now)
        flux_north = north_edge * (jnp.roll(field_now, -1, axis=-2) - field_now)
        increment_field = flux_east - jnp.roll(flux_east, 1, axis=-1) + flux_north - jnp.roll(flux_north, 1, axis=-2)
        return field_now + increment_field
    return lax.fori_loop(0, ITERS, one_step, field)


def reference(control, perturb, obs_count, obs_kind, obs_table, band_filter, diffusivity):
    highest_level = lax.Precision.HIGHEST
    east_edge, north_edge = edge_coeffs(diffusivity)
    smooth = diffuse(control, east_edge, north_edge)
    filtered_field = jnp.einsum("lm,kmij->klij", band_filter, smooth, precision=highest_level)
    increment_field = jnp.einsum("kvlij,klij->vlij", perturb, filtered_field, precision=highest_level)
    looked_up = obs_table[obs_kind].reshape(NLAT, NLON, 3, LEVELS)
    weights = jnp.transpose(looked_up, (2, 3, 0, 1)) * obs_count.astype(jnp.float32)[None, None, :, :]
    weighted_field = weights * increment_field
    adjoint_field = jnp.einsum("kvlij,vlij->klij", perturb, weighted_field, precision=highest_level)
    lifted = jnp.einsum("lm,klij->kmij", band_filter, adjoint_field, precision=highest_level)
    return control + diffuse(lifted, east_edge, north_edge)
```

```python
import jax
import jax.numpy as jnp
from jax import lax
from jax.experimental import pallas as pl
from jax.experimental.pallas import tpu as pltpu
from jax.sharding import PartitionSpec as P

ITERS = 16
SUB = 8
VMEM = pl.BlockSpec(memory_space=pltpu.VMEM)
HIGHEST = lax.Precision.HIGHEST


def coefficients(diff_ref, east, north, steps, lanes):
    lane = lax.broadcasted_iota(jnp.int32, (SUB, lanes), 1)
    cells = [diff_ref[pl.ds(r, SUB, stride=steps), :] for r in range(steps)]
    wrapped = pltpu.roll(cells[0], SUB - 1, 0)
    for r in range(steps):
        here = cells[r]
        there = cells[r + 1] if r + 1 < steps else wrapped
        east[r] = 0.5 * (here + there)
        up = 0.5 * (here + pltpu.roll(here, lanes - 1, 1))
        north[r] = jnp.where(lane < lanes - 1, up, jnp.zeros_like(up))


def diffuse_in_place(field, east, north, planes, steps, lanes):
    def one_step(step_index, carry):
        first = [field[q, 0] for q in range(planes)]
        ahead = [pltpu.roll(f, SUB - 1, 0) for f in first]
        here = list(first)
        before = [
            pltpu.roll(east[steps - 1] * (ahead[q] - field[q, steps - 1]), 1, 0)
            for q in range(planes)
        ]
        for r in range(steps):
            east_r, north_r = east[r], north[r]
            for q in range(planes):
                there = field[q, r + 1] if r + 1 < steps else ahead[q]
                flux_east = east_r * (there - here[q])
                flux_north = north_r * (pltpu.roll(here[q], lanes - 1, 1) - here[q])
                change = (flux_east - before[q]) + (flux_north - pltpu.roll(flux_north, 1, 1))
                field[q, r] = here[q] + change
                before[q] = flux_east
                here[q] = there
        return carry

    lax.fori_loop(0, ITERS, one_step, 0)


def spread_out(control_ref, diff_ref, out_ref, east, north, field, plain):
    planes, lon, lat = control_ref.shape
    steps = lon // SUB
    rows = lat // out_ref.shape[0]
    coefficients(diff_ref, east, north, steps, lat)
    for q in range(planes):
        for r in range(steps):
            field[q, r] = control_ref[q, pl.ds(r, SUB, stride=steps), :]
    diffuse_in_place(field, east, north, planes, steps, lat)
    for q in range(planes):
        for r in range(steps):
            plain[q, pl.ds(r, SUB, stride=steps), :] = field[q, r]
        for start in range(0, lon, 128):
            width = min(128, lon - start)
            turned = plain[q, start : start + 128, :].T
            for d in range(lat // rows):
                out_ref[d, rows * q : rows * q + rows, start : start + width] = turned[
                    rows * d : rows * d + rows, :width
                ]


def gather_in(pieces_ref, control_ref, diff_ref, out_ref, east, north, field, plain, whole):
    planes, lon, lat = control_ref.shape
    steps = lon // SUB
    devices = pieces_ref.shape[0]
    rows = lat // devices
    coefficients(diff_ref, east, north, steps, lat)
    for q in range(planes):
        for d in range(devices):
            whole[rows * d : rows * d + rows, :lon] = pieces_ref[d, rows * q : rows * q + rows, :]
        for start in range(0, lon, 128):
            plain[q, start : start + 128, :] = whole[:, start : start + 128].T
        for r in range(steps):
            field[q, r] = plain[q, pl.ds(r, SUB, stride=steps), :]
    diffuse_in_place(field, east, north, planes, steps, lat)
    for q in range(planes):
        for r in range(steps):
            place = pl.ds(r, SUB, stride=steps)
            out_ref[q, place, :] = control_ref[q, place, :] + field[q, r]


def partial_sums(core_ref, band_ref, first_ref, second_ref, perturb_ref, *rest):
    outs, filtered = rest[:6], rest[6]
    rows = first_ref.shape[0]
    half = rows // 2
    filtered[0] = first_ref[...]
    filtered[1] = jnp.dot(
        band_ref[...], second_ref[...], precision=HIGHEST, preferred_element_type=jnp.float32
    )
    core = core_ref[0]
    for side in range(2):
        base = (core if side else 1 - core) * half

        def body(t, carry, side=side, base=base):
            at = pl.ds(pl.multiple_of(base + t * SUB, SUB), SUB)
            to = pl.ds(pl.multiple_of(t * SUB, SUB), SUB)
            f0, f1 = filtered[0, at, :], filtered[1, at, :]
            for v in range(3):
                outs[3 * side + v][to, :] = (
                    perturb_ref[0, v, at, :] * f0 + perturb_ref[1, v, at, :] * f1
                )
            return carry

        lax.fori_loop(0, half // SUB, body, 0)


def lift(core_ref, band_ref, perturb_ref, *rest):
    own, other, out_ref, adjoint = rest[:3], rest[3:6], rest[6], rest[7]
    rows = out_ref.shape[0]
    half = rows // 2
    core = core_ref[0]
    for side in range(2):
        base = (core if side == 0 else 1 - core) * half
        weighted = own if side == 0 else other

        def body(t, carry, base=base, weighted=weighted):
            at = pl.ds(pl.multiple_of(base + t * SUB, SUB), SUB)
            to = pl.ds(pl.multiple_of(t * SUB, SUB), SUB)
            total = perturb_ref[0, at, :] * weighted[0][to, :]
            for v in (1, 2):
                total = total + perturb_ref[v, at, :] * weighted[v][to, :]
            adjoint[at, :] = total
            return carry

        lax.fori_loop(0, half // SUB, body, 0)
    out_ref[...] = jnp.dot(
        band_ref[...], adjoint[...], precision=HIGHEST, preferred_element_type=jnp.float32
    )


def call(kernel, out_shape, scratch, flops, moved, smem_first=False):
    def run(*args):
        specs = [VMEM] * len(args)
        if smem_first:
            specs[0] = pl.BlockSpec(memory_space=pltpu.SMEM)
        return pl.pallas_call(
            kernel,
            out_shape=out_shape,
            in_specs=specs,
            out_specs=jax.tree.map(lambda _: VMEM, out_shape),
            scratch_shapes=scratch,
            cost_estimate=pl.CostEstimate(flops=flops, bytes_accessed=moved, transcendentals=0),
            compiler_params=pltpu.CompilerParams(vmem_limit_bytes=40 << 20),
        )(*args)

    return run


def f32(*shape):
    return jax.ShapeDtypeStruct(shape, jnp.float32)


def local(control, perturb, obs_count, obs_kind, obs_table, band_filter, diffusivity):
    members, planes, lat, lon = control.shape
    kinds = obs_table.shape[0]
    variables, levels, rows = perturb.shape[1:4]
    devices = lax.axis_size("wide")
    steps = lon // SUB
    flat = levels * rows
    half = flat // 2
    padded = -(-lon // 128) * 128
    control_t = jnp.swapaxes(control, 2, 3)
    diff_t = jnp.swapaxes(diffusivity, 0, 1)
    core = lax.axis_index("mem") % 2

    coefs = [pltpu.VMEM((steps, SUB, lat), jnp.float32)] * 2
    field = pltpu.VMEM((planes, steps, SUB, lat), jnp.float32)
    plain = pltpu.VMEM((planes, padded, lat), jnp.float32)
    whole = pltpu.VMEM((lat, padded), jnp.float32)
    work = planes * lat * lon * ITERS * 8
    size = planes * lat * lon * 4

    def to_rows(k):
        sent = call(spread_out, f32(devices, planes * rows, lon), [*coefs, field, plain], work, 2 * size)(
            control_t[k], diff_t
        )
        got = lax.all_to_all(sent, "wide", 0, 0, tiled=True)
        return got.reshape(flat, lon)

    def to_planes(k, lifted):
        got = lax.all_to_all(
            lifted.reshape(devices, planes * rows, lon), "wide", 0, 0, tiled=True
        )
        return call(gather_in, f32(planes, lon, lat), [*coefs, field, plain, whole], work, 3 * size)(
            got, control_t[k], diff_t
        )

    smooth = [to_rows(k) for k in range(members)]

    eye = jnp.eye(rows, dtype=jnp.float32)
    band = (band_filter[:, None, :, None] * eye[None, :, None, :]).reshape(flat, flat)
    band_t = (band_filter.T[:, None, :, None] * eye[None, :, None, :]).reshape(flat, flat)
    perturb_rows = perturb.reshape(members, variables, flat, lon)

    kind_rows = lax.broadcasted_iota(jnp.int32, (kinds,) + obs_kind.shape, 0)
    one_hot = jnp.where(obs_kind[None] == kind_rows, obs_count[None], 0).astype(jnp.float32)
    table = lax.dynamic_slice_in_dim(
        obs_table.reshape(kinds, variables, levels), core * (levels // 2), levels // 2, 2
    )
    weights = jnp.einsum("kvl,kij->vlij", table, one_hot, precision=HIGHEST)
    weights = weights.reshape(variables, half, lon)

    filtered = jnp.dot(band, smooth[0], precision=HIGHEST)
    scalar = core.astype(jnp.int32).reshape(1)
    parts = call(
        partial_sums,
        [f32(half, lon)] * 6,
        [pltpu.VMEM((members, flat, lon), jnp.float32)],
        2 * flat * flat * lon,
        12 * flat * lon * 4,
        True,
    )(scalar, band, filtered, smooth[1], perturb_rows)

    other_core = [(i, i ^ 1) for i in range(4)]
    next_chip = [(i, i ^ 2) for i in range(4)]
    own, other = [], []
    for v in range(variables):
        on_chip = parts[3 + v] + lax.ppermute(parts[v], "mem", other_core)
        total = on_chip + lax.ppermute(on_chip, "mem", next_chip)
        own.append(weights[v] * total)
        other.append(lax.ppermute(own[v], "mem", other_core))

    out = []
    for k in range(members):
        lifted = call(
            lift,
            f32(flat, lon),
            [pltpu.VMEM((flat, lon), jnp.float32)],
            2 * flat * flat * lon,
            8 * flat * lon * 4,
            True,
        )(scalar, band_t, perturb_rows[k], *own, *other)
        out.append(to_planes(k, lifted))
    return jnp.swapaxes(jnp.stack(out), 2, 3)


def solution(mesh):
    placed = (
        P("mem", "wide", None, None),
        P("mem", None, None, "wide", None),
        P("wide", None),
        P("wide", None),
        P(),
        P(),
        P(),
    )
    return jax.shard_map(
        local, mesh=mesh, in_specs=placed, out_specs=P("mem", "wide", None, None), check_vma=False
    )
```

```python
import jax
import jax.numpy as jnp
from jax import lax
from jax.experimental import pallas as pl
from jax.experimental.pallas import tpu as pltpu
from jax.sharding import PartitionSpec as P

ITERS = 16
SUB = 8
LANES = 128
VMEM = pl.BlockSpec(memory_space=pltpu.VMEM)
SMEM = pl.BlockSpec(memory_space=pltpu.SMEM)
HIGHEST = lax.Precision.HIGHEST


def dot(a, b, contract=((1,), (0,))):
    return lax.dot_general(
        a, b, (contract, ((), ())), precision=HIGHEST, preferred_element_type=jnp.float32
    )


def iota(shape, dim):
    return lax.broadcasted_iota(jnp.int32, shape, dim)


def ones_where(mask):
    return jnp.where(mask, 1.0, 0.0).astype(jnp.float32)


def blocks_of(lon):
    return [(start, min(LANES, lon - start)) for start in range(0, lon, LANES)]


def coefficients(diff_ref, east, north, turned, flat):
    rows, steps = east.shape[:2]
    lon, lat = diff_ref.shape
    blocks = lat // rows
    copies = LANES // blocks
    for start, width in blocks_of(lon):
        turned[start // LANES, :lat, :width] = diff_ref[start : start + width, :].T
    for i in range(rows):
        for start, width in blocks_of(lon):
            picked = turned[start // LANES, pl.ds(i, blocks, stride=rows), :]
            flat[i, start : start + LANES, :] = jnp.concatenate([picked] * copies, 0).T
    edge = lax.rem(iota((SUB, LANES), 1), blocks) == blocks - 1
    first = [flat[i, pl.ds(0, SUB, stride=steps), :] for i in range(rows)]
    here = list(first)
    for r in range(steps):
        for i in range(rows):
            if r + 1 < steps:
                there = flat[i, pl.ds(r + 1, SUB, stride=steps), :]
            else:
                there = pltpu.roll(first[i], SUB - 1, 0)
            east[i, r] = 0.5 * (here[i] + there)
            if i + 1 < rows:
                north[i, r] = 0.5 * (here[i] + here[i + 1])
            else:
                up = 0.5 * (here[i] + pltpu.roll(start_of_row, LANES - 1, 1))
                north[i, r] = jnp.where(edge, jnp.zeros_like(up), up)
            if i == 0:
                start_of_row = here[0]
            here[i] = there if i else here[i]
            if i == 0:
                next_of_row = there
        here[0] = next_of_row


def diffuse_in_place(field, east, north):
    rows, steps = field.shape[:2]

    def one_step(step_index, carry):
        here = [field[i, 0] for i in range(rows)]
        ahead = [pltpu.roll(f, SUB - 1, 0) for f in here]
        before = [
            pltpu.roll(east[i, steps - 1] * (ahead[i] - field[i, steps - 1]), 1, 0)
            for i in range(rows)
        ]
        for r in range(steps):
            there = [field[i, r + 1] if r + 1 < steps else ahead[i] for i in range(rows)]
            up = here[1:] + [pltpu.roll(here[0], LANES - 1, 1)]
            flux_north = [north[i, r] * (up[i] - here[i]) for i in range(rows)]
            down = [pltpu.roll(flux_north[-1], 1, 1)] + flux_north[:-1]
            for i in range(rows):
                flux_east = east[i, r] * (there[i] - here[i])
                field[i, r] = here[i] + ((flux_east - before[i]) + (flux_north[i] - down[i]))
                before[i] = flux_east
            here = there
        return carry

    lax.fori_loop(0, ITERS, one_step, 0)


def spread_out(control_ref, diff_ref, a_ref, b_ref, east, north, field, turned, flat):
    planes, lon, lat = control_ref.shape
    rows, steps = field.shape[:2]
    blocks = lat // rows
    tiles = turned.shape[0]
    turned[tiles - 1] = jnp.zeros(turned.shape[1:], jnp.float32)
    flat[:, (tiles - 1) * LANES :, :] = jnp.zeros((rows, LANES, LANES), jnp.float32)
    half = tiles // 2
    coefficients(diff_ref, east, north, turned, flat)
    for q in range(planes):
        for start, width in blocks_of(lon):
            turned[start // LANES, lat * q : lat * q + lat, :width] = control_ref[
                q, start : start + width, :
            ].T
    for i in range(rows):
        for start, width in blocks_of(lon):
            picked = [
                turned[start // LANES, pl.ds(lat * q + i, blocks, stride=rows), :]
                for q in range(planes)
            ]
            flat[i, start : start + LANES, :] = jnp.concatenate(picked, 0).T
        for r in range(steps):
            field[i, r] = flat[i, pl.ds(r, SUB, stride=steps), :]
    diffuse_in_place(field, east, north)
    for i in range(rows):
        for r in range(steps):
            flat[i, pl.ds(r, SUB, stride=steps), :] = field[i, r]
        for start, width in blocks_of(lon):
            block = flat[i, start : start + LANES, :].T
            out_ref, tile = (a_ref, b_ref)[start // LANES // half], start // LANES % half
            for q in range(planes):
                row = (tile * planes + q) * rows + i
                out_ref[pl.ds(row, blocks, stride=half * planes * rows), :] = block[
                    q * blocks : (q + 1) * blocks, :
                ]


def gather_in(a_ref, b_ref, control_ref, east, north, out_ref, field, turned, flat):
    planes, lon, lat = control_ref.shape
    rows, steps = field.shape[:2]
    blocks = lat // rows
    half = turned.shape[0] // 2
    for i in range(rows):
        for start, width in blocks_of(lon):
            in_ref, tile = (a_ref, b_ref)[start // LANES // half], start // LANES % half
            picked = [
                in_ref[
                    pl.ds((tile * planes + q) * rows + i, blocks, stride=half * planes * rows), :
                ]
                for q in range(planes)
            ]
            flat[i, start : start + LANES, :] = jnp.concatenate(picked, 0).T
        for r in range(steps):
            field[i, r] = flat[i, pl.ds(r, SUB, stride=steps), :]
    diffuse_in_place(field, east, north)
    for i in range(rows):
        for r in range(steps):
            flat[i, pl.ds(r, SUB, stride=steps), :] = field[i, r]
        for start, width in blocks_of(lon):
            block = flat[i, start : start + LANES, :].T
            for q in range(planes):
                turned[start // LANES, pl.ds(lat * q + i, blocks, stride=rows), :] = block[
                    q * blocks : (q + 1) * blocks, :
                ]
    for q in range(planes):
        for start, width in blocks_of(lon):
            back = turned[start // LANES, lat * q : lat * q + lat, :].T
            out_ref[q, start : start + width, :] = (
                control_ref[q, start : start + width, :] + back[:width, :]
            )


def prepare(core_ref, filter_ref, table_ref, count_ref, kind_ref, band_ref, band_t_ref, weight_ref):
    levels = filter_ref.shape[0]
    flat = band_ref.shape[0]
    rows = flat // levels
    kinds, columns = table_ref.shape
    lon = count_ref.shape[1]
    own = weight_ref.shape[0]
    variables = columns // levels
    share = own // variables // rows
    spread = ones_where(iota((flat, levels), 0) // rows == iota((flat, levels), 1))
    spread_t = ones_where(iota((levels, flat), 1) // rows == iota((levels, flat), 0))
    same = lax.rem(iota((flat, flat), 0), rows) == lax.rem(iota((flat, flat), 1), rows)
    weight = filter_ref[...]
    band_ref[...] = jnp.where(same, dot(dot(spread, weight), spread_t), 0.0)
    band_t_ref[...] = jnp.where(same, dot(dot(spread, weight, ((1,), (1,))), spread_t), 0.0)
    row = iota((own, columns), 0)
    column = (
        row // (share * rows) * levels
        + core_ref[0] * share
        + lax.rem(row // rows, share)
    )
    picked = dot(ones_where(column == iota((own, columns), 1)), table_ref[...], ((1,), (1,)))
    wide = kinds * rows
    each = ones_where(iota((kinds, wide), 1) // rows == iota((kinds, wide), 0))
    match = lax.rem(iota((own, wide), 0), rows) == lax.rem(iota((own, wide), 1), rows)
    table = jnp.where(match, dot(picked, each), 0.0)
    repeat = ones_where(lax.rem(iota((wide, rows), 0), rows) == iota((wide, rows), 1))
    kind = dot(repeat, kind_ref[...].astype(jnp.float32))
    count = dot(repeat, count_ref[...].astype(jnp.float32))
    which = (iota((wide, lon), 0) // rows).astype(jnp.float32)
    weight_ref[:, :lon] = dot(table, jnp.where(kind == which, count, 0.0))
    weight_ref[:, lon:] = jnp.zeros((own, weight_ref.shape[1] - lon), jnp.float32)


def relayout(perturb_ref, out_ref):
    levels, rows, lon = perturb_ref.shape
    out_ref[:, lon:] = jnp.zeros((levels * rows, out_ref.shape[1] - lon), jnp.float32)
    pair = SUB // rows
    for t in range(levels // pair):
        out_ref[SUB * t : SUB * t + SUB, :lon] = jnp.concatenate(
            [perturb_ref[pair * t + u] for u in range(pair)], 0
        )


def partial_sums(offset, core_ref, band_ref, pieces_ref, perturb_ref, send_ref, keep_ref, filtered):
    devices, tiles, height = pieces_ref.shape[:3]
    width = tiles * LANES
    members, variables, flat = perturb_ref.shape[:3]
    piece = height // members
    half = flat // 2
    for k in range(members):
        mine = [
            pieces_ref[:, t, piece * k : piece * k + piece, :].reshape(flat, LANES)
            for t in range(tiles)
        ]
        filtered[k] = dot(band_ref[...], jnp.concatenate(mine, 1))
    core = core_ref[0]
    for side, out_ref in enumerate((send_ref, keep_ref)):
        base = (core if side else 1 - core) * half

        def body(t, carry, out_ref=out_ref, base=base):
            at = pl.ds(pl.multiple_of(base + t * SUB, SUB), SUB)
            fields = [filtered[k, at, :] for k in range(members)]
            for v in range(variables):
                total = perturb_ref[0, v, at, offset : offset + width] * fields[0]
                for k in range(1, members):
                    total = total + perturb_ref[k, v, at, offset : offset + width] * fields[k]
                out_ref[pl.ds(pl.multiple_of(v * half + t * SUB, SUB), SUB), :] = total
            return carry

        lax.fori_loop(0, half // SUB, body, 0)


def lift(offset, core_ref, band_ref, own_ref, other_ref, perturb_ref, out_ref, adjoint):
    devices, tiles, height = out_ref.shape[:3]
    width = tiles * LANES
    members, variables, flat = perturb_ref.shape[:3]
    piece = height // members
    half = flat // 2
    core = core_ref[0]
    for side, weighted in enumerate((own_ref, other_ref)):
        base = (core if side == 0 else 1 - core) * half

        def body(t, carry, weighted=weighted, base=base):
            at = pl.ds(pl.multiple_of(base + t * SUB, SUB), SUB)
            parts = [
                weighted[pl.ds(pl.multiple_of(v * half + t * SUB, SUB), SUB), :]
                for v in range(variables)
            ]
            for k in range(members):
                total = perturb_ref[k, 0, at, offset : offset + width] * parts[0]
                for v in range(1, variables):
                    total = total + perturb_ref[k, v, at, offset : offset + width] * parts[v]
                adjoint[k, at, :] = total
            return carry

        lax.fori_loop(0, half // SUB, body, 0)
    for k in range(members):
        whole = dot(band_ref[...], adjoint[k])
        for t in range(tiles):
            out_ref[:, t, piece * k : piece * k + piece, :] = whole[
                :, t * LANES : (t + 1) * LANES
            ].reshape(devices, piece, LANES)


def call(kernel, out_shape, scratch, flops, moved, smem_first=False, limit=16):
    def run(*args):
        specs = [VMEM] * len(args)
        if smem_first:
            specs[0] = SMEM
        return pl.pallas_call(
            kernel,
            out_shape=out_shape,
            in_specs=specs,
            out_specs=jax.tree.map(lambda _: VMEM, out_shape),
            scratch_shapes=scratch,
            cost_estimate=pl.CostEstimate(flops=flops, bytes_accessed=moved, transcendentals=0),
            compiler_params=pltpu.CompilerParams(vmem_limit_bytes=limit << 20),
        )(*args)

    return run


def f32(*shape):
    return jax.ShapeDtypeStruct(shape, jnp.float32)


def local(control, perturb, obs_count, obs_kind, obs_table, band_filter, diffusivity):
    members, level_planes, lat, lon = control.shape
    variables, levels, rows = perturb.shape[1:4]
    devices = lax.axis_size("wide")
    planes = members * level_planes
    steps = lon // SUB
    flat = levels * rows
    half = flat // 2
    padded = -(-lon // (2 * LANES)) * 2 * LANES
    width = padded // 2
    height = planes * rows
    control_t = jnp.swapaxes(control, 2, 3).reshape(planes, lon, lat)
    diff_t = jnp.swapaxes(diffusivity, 0, 1)
    core = (lax.axis_index("mem") % 2).astype(jnp.int32).reshape(1)

    coefs = f32(rows, steps, SUB, LANES)
    field = pltpu.VMEM(coefs.shape, jnp.float32)
    tiles = width // LANES
    turned = pltpu.VMEM((2 * tiles, planes * lat, LANES), jnp.float32)
    flat_field = pltpu.VMEM((rows, padded, LANES), jnp.float32)
    work = planes * lat * lon * ITERS * 8
    size = planes * lat * lon * 4

    sent = f32(devices * tiles * height, LANES)
    sent_a, sent_b, east, north = call(
        spread_out, [sent, sent, coefs, coefs], [field, turned, flat_field], work, 2 * size, limit=20
    )(control_t, diff_t)

    def exchange(sent):
        return lax.all_to_all(sent.reshape(devices, tiles, height, LANES), "wide", 0, 0, tiled=True)

    pieces = [exchange(sent_a), exchange(sent_b)]

    band, band_t, weights = call(
        prepare,
        [f32(flat, flat), f32(flat, flat), f32(variables * half, padded)],
        [],
        1 << 28,
        4 << 20,
        True,
    )(core, band_filter, obs_table, obs_count, obs_kind)
    perturb_rows = pl.pallas_call(
        relayout,
        out_shape=f32(members * variables, flat, padded),
        grid=(members * variables,),
        in_specs=[pl.BlockSpec((None, levels, rows, lon), lambda g: (g, 0, 0, 0))],
        out_specs=pl.BlockSpec((None, flat, padded), lambda g: (g, 0, 0)),
        cost_estimate=pl.CostEstimate(flops=1 << 20, bytes_accessed=6 * size, transcendentals=0),
        compiler_params=pltpu.CompilerParams(vmem_limit_bytes=8 << 20),
    )(perturb.reshape(members * variables, levels, rows, lon))
    perturb_rows = perturb_rows.reshape(members, variables, flat, padded)

    other_core = [(i, i ^ 1) for i in range(4)]
    next_chip = [(i, i ^ 2) for i in range(4)]
    part = f32(variables * half, width)
    lifted = []
    for h in range(2):
        offset = h * width

        def sums(*refs, offset=offset):
            partial_sums(offset, *refs)

        def lifting(*refs, offset=offset):
            lift(offset, *refs)

        scratch = [pltpu.VMEM((members, flat, width), jnp.float32)]
        send, keep = call(sums, [part, part], scratch, 1 << 29, 4 * size, True)(
            core, band, pieces[h], perturb_rows
        )
        on_chip = keep + lax.ppermute(send, "mem", other_core)
        total = on_chip + lax.ppermute(on_chip, "mem", next_chip)
        own = weights[:, offset : offset + width] * total
        other = lax.ppermute(own, "mem", other_core)
        out = call(lifting, f32(devices, tiles, height, LANES), scratch, 1 << 29, 4 * size, True)(
            core, band_t, own, other, perturb_rows
        )
        lifted.append(exchange(out).reshape(sent.shape))

    out = call(
        gather_in, f32(planes, lon, lat), [field, turned, flat_field], work, 3 * size, limit=20
    )(*lifted, control_t, east, north)
    return jnp.swapaxes(out.reshape(members, level_planes, lon, lat), 2, 3)


def solution(mesh):
    placed = (
        P("mem", "wide", None, None),
        P("mem", None, None, "wide", None),
        P("wide", None),
        P("wide", None),
        P(),
        P(),
        P(),
    )
    return jax.shard_map(
        local, mesh=mesh, in_specs=placed, out_specs=P("mem", "wide", None, None), check_vma=False
    )
```

```python
import jax
import jax.numpy as jnp
from jax import lax
from jax.experimental import pallas as pl
from jax.experimental.pallas import tpu as pltpu
from jax.sharding import PartitionSpec as P


ITERS = 16
SUB = 8
LANES = 128
VMEM = pl.BlockSpec(memory_space=pltpu.VMEM)
SMEM = pl.BlockSpec(memory_space=pltpu.SMEM)
HBM = pl.BlockSpec(memory_space=pltpu.HBM)
HIGHEST = lax.Precision.HIGHEST


def dot(a, b, contract=((1,), (0,))):
    return lax.dot_general(
        a, b, (contract, ((), ())), precision=HIGHEST, preferred_element_type=jnp.float32
    )


def iota(shape, dim):
    return lax.broadcasted_iota(jnp.int32, shape, dim)


def ones_where(mask):
    return jnp.where(mask, 1.0, 0.0).astype(jnp.float32)


def blocks_of(lon):
    return [(start, min(LANES, lon - start)) for start in range(0, lon, LANES)]


def coefficients(diff_ref, east, north, turned, flat):
    rows, steps = east.shape[:2]
    lon, lat = diff_ref.shape
    blocks = lat // rows
    copies = LANES // blocks
    for start, width in blocks_of(lon):
        turned[start // LANES, :lat, :width] = diff_ref[start : start + width, :].T
    for i in range(rows):
        for start, width in blocks_of(lon):
            picked = turned[start // LANES, pl.ds(i, blocks, stride=rows), :]
            flat[i, start : start + LANES, :] = jnp.concatenate([picked] * copies, 0).T
    edge = lax.rem(iota((SUB, LANES), 1), blocks) == blocks - 1
    first = [flat[i, pl.ds(0, SUB, stride=steps), :] for i in range(rows)]
    here = list(first)
    for r in range(steps):
        for i in range(rows):
            if r + 1 < steps:
                there = flat[i, pl.ds(r + 1, SUB, stride=steps), :]
            else:
                there = pltpu.roll(first[i], SUB - 1, 0)
            east[i, r] = 0.5 * (here[i] + there)
            if i + 1 < rows:
                north[i, r] = 0.5 * (here[i] + here[i + 1])
            else:
                up = 0.5 * (here[i] + pltpu.roll(start_of_row, LANES - 1, 1))
                north[i, r] = jnp.where(edge, jnp.zeros_like(up), up)
            if i == 0:
                start_of_row = here[0]
            here[i] = there if i else here[i]
            if i == 0:
                next_of_row = there
        here[0] = next_of_row


def diffuse_in_place(field, east, north):
    rows, steps = field.shape[:2]

    def one_step(step_index, carry):
        here = [field[i, 0] for i in range(rows)]
        ahead = [pltpu.roll(f, SUB - 1, 0) for f in here]
        before = [
            pltpu.roll(east[i, steps - 1] * (ahead[i] - field[i, steps - 1]), 1, 0)
            for i in range(rows)
        ]
        for r in range(steps):
            there = [field[i, r + 1] if r + 1 < steps else ahead[i] for i in range(rows)]
            up = here[1:] + [pltpu.roll(here[0], LANES - 1, 1)]
            flux_north = [north[i, r] * (up[i] - here[i]) for i in range(rows)]
            down = [pltpu.roll(flux_north[-1], 1, 1)] + flux_north[:-1]
            for i in range(rows):
                flux_east = east[i, r] * (there[i] - here[i])
                field[i, r] = here[i] + ((flux_east - before[i]) + (flux_north[i] - down[i]))
                before[i] = flux_east
            here = there
        return carry

    lax.fori_loop(0, ITERS, one_step, 0)


def spread_out(
    control_hbm, diff_ref, sent_ref, east_hbm, north_hbm,
    control, east, north, field, turned, flat, sems,
):
    planes, lon, lat = control.shape
    rows, steps = field.shape[:2]
    blocks = lat // rows
    tiles = turned.shape[0]
    fetch = pltpu.make_async_copy(control_hbm, control, sems.at[0])
    fetch.start()
    turned[tiles - 1] = jnp.zeros(turned.shape[1:], jnp.float32)
    flat[:, (tiles - 1) * LANES :, :] = jnp.zeros((rows, LANES, LANES), jnp.float32)
    coefficients(diff_ref, east, north, turned, flat)
    keep_east = pltpu.make_async_copy(east, east_hbm, sems.at[1])
    keep_north = pltpu.make_async_copy(north, north_hbm, sems.at[2])
    keep_east.start()
    keep_north.start()
    fetch.wait()
    for q in range(planes):
        for start, width in blocks_of(lon):
            turned[start // LANES, lat * q : lat * q + lat, :width] = control[
                q, start : start + width, :
            ].T
    for i in range(rows):
        for start, width in blocks_of(lon):
            picked = [
                turned[start // LANES, pl.ds(lat * q + i, blocks, stride=rows), :]
                for q in range(planes)
            ]
            flat[i, start : start + LANES, :] = jnp.concatenate(picked, 0).T
        for r in range(steps):
            field[i, r] = flat[i, pl.ds(r, SUB, stride=steps), :]
    diffuse_in_place(field, east, north)
    for i in range(rows):
        for r in range(steps):
            flat[i, pl.ds(r, SUB, stride=steps), :] = field[i, r]
        for start, width in blocks_of(lon):
            block = flat[i, start : start + LANES, :].T
            for q in range(planes):
                row = (start // LANES * planes + q) * rows + i
                sent_ref[pl.ds(row, blocks, stride=tiles * planes * rows), :] = block[
                    q * blocks : (q + 1) * blocks, :
                ]
    keep_east.wait()
    keep_north.wait()


def gather_in(
    a_ref, b_ref, control_hbm, east_hbm, north_hbm, out_hbm,
    control, east, north, field, turned, flat, sems,
):
    planes, lon, lat = control.shape
    rows, steps = field.shape[:2]
    blocks = lat // rows
    tiles_a = a_ref.shape[0] // (blocks * planes * rows)
    tiles_b = b_ref.shape[0] // (blocks * planes * rows)
    fetches = [
        pltpu.make_async_copy(source, target, sems.at[n])
        for n, (source, target) in enumerate(
            ((east_hbm, east), (north_hbm, north), (control_hbm, control))
        )
    ]
    for fetch in fetches:
        fetch.start()
    for i in range(rows):
        for start, width in blocks_of(lon):
            in_ref, tile, tiles = a_ref, start // LANES, tiles_a
            if tile >= tiles_a:
                in_ref, tile, tiles = b_ref, tile - tiles_a, tiles_b
            picked = [
                in_ref[
                    pl.ds((tile * planes + q) * rows + i, blocks, stride=tiles * planes * rows), :
                ]
                for q in range(planes)
            ]
            flat[i, start : start + LANES, :] = jnp.concatenate(picked, 0).T
        for r in range(steps):
            field[i, r] = flat[i, pl.ds(r, SUB, stride=steps), :]
    for fetch in fetches:
        fetch.wait()
    diffuse_in_place(field, east, north)
    for i in range(rows):
        for r in range(steps):
            flat[i, pl.ds(r, SUB, stride=steps), :] = field[i, r]
        for start, width in blocks_of(lon):
            block = flat[i, start : start + LANES, :].T
            for q in range(planes):
                turned[start // LANES, pl.ds(lat * q + i, blocks, stride=rows), :] = block[
                    q * blocks : (q + 1) * blocks, :
                ]
    stores = []
    for q in range(planes):
        for start, width in blocks_of(lon):
            back = turned[start // LANES, lat * q : lat * q + lat, :].T
            place = pl.ds(start, width)
            control[q, place, :] = control[q, place, :] + back[:width, :]
        stores.append(pltpu.make_async_copy(control.at[q], out_hbm.at[q], sems.at[3 + q]))
        stores[-1].start()
    for store in stores:
        store.wait()


def prepare(core_ref, filter_ref, table_ref, count_ref, kind_ref, band_ref, band_t_ref, *weight_refs):
    levels = filter_ref.shape[0]
    flat = band_ref.shape[0]
    rows = flat // levels
    kinds, columns = table_ref.shape
    lon = count_ref.shape[1]
    own, width = weight_refs[0].shape
    variables = columns // levels
    share = own // variables // rows
    spread = ones_where(iota((flat, levels), 0) // rows == iota((flat, levels), 1))
    spread_t = ones_where(iota((levels, flat), 1) // rows == iota((levels, flat), 0))
    same = lax.rem(iota((flat, flat), 0), rows) == lax.rem(iota((flat, flat), 1), rows)
    weight = filter_ref[...]
    band_ref[...] = jnp.where(same, dot(dot(spread, weight), spread_t), 0.0)
    band_t_ref[...] = jnp.where(same, dot(dot(spread, weight, ((1,), (1,))), spread_t), 0.0)
    row = iota((own, columns), 0)
    column = (
        row // (share * rows) * levels
        + core_ref[0] * share
        + lax.rem(row // rows, share)
    )
    picked = dot(ones_where(column == iota((own, columns), 1)), table_ref[...], ((1,), (1,)))
    wide = kinds * rows
    each = ones_where(iota((kinds, wide), 1) // rows == iota((kinds, wide), 0))
    match = lax.rem(iota((own, wide), 0), rows) == lax.rem(iota((own, wide), 1), rows)
    table = jnp.where(match, dot(picked, each), 0.0)
    repeat = ones_where(lax.rem(iota((wide, rows), 0), rows) == iota((wide, rows), 1))
    kind = dot(repeat, kind_ref[...].astype(jnp.float32))
    count = dot(repeat, count_ref[...].astype(jnp.float32))
    which = (iota((wide, lon), 0) // rows).astype(jnp.float32)
    chosen = jnp.where(kind == which, count, 0.0)
    for h, weight_ref in enumerate(weight_refs):
        used = min(width, lon - h * width)
        if used < width:
            weight_ref[:, used:] = jnp.zeros((own, width - used), jnp.float32)
        weight_ref[:, :used] = dot(table, chosen[:, h * width : h * width + used])


def level_pair(perturb_ref, k, v, level, rows):
    return jnp.concatenate([perturb_ref[k, v, level + u] for u in range(SUB // rows)], 0)


def partial_sums(core_ref, band_ref, pieces_ref, perturb_ref, send_ref, keep_ref, filtered):
    members, variables, levels, rows = perturb_ref.shape[:4]
    flat = levels * rows
    piece = pieces_ref.shape[1] // members
    mine = [
        pieces_ref[:, piece * k : piece * k + piece, :].reshape(flat, LANES)
        for k in range(members)
    ]
    filtered[...] = dot(band_ref[...], jnp.concatenate(mine, 1))
    core = core_ref[0]
    half = flat // 2
    for side, out_ref in enumerate((send_ref, keep_ref)):
        part = core if side else 1 - core
        for t in range(half // SUB):
            at = pl.ds(pl.multiple_of(part * half + t * SUB, SUB), SUB)
            level = part * (levels // 2) + t * (SUB // rows)
            fields = [filtered[at, LANES * k : LANES * (k + 1)] for k in range(members)]
            for v in range(variables):
                total = level_pair(perturb_ref, 0, v, level, rows) * fields[0]
                for k in range(1, members):
                    total = total + level_pair(perturb_ref, k, v, level, rows) * fields[k]
                out_ref[v * half + t * SUB : v * half + t * SUB + SUB, :] = total


def lift(core_ref, band_ref, own_ref, other_ref, perturb_ref, *rest):
    out_ref, adjoint = rest[-2:]
    members, variables, levels, rows = perturb_ref.shape[:4]
    flat = levels * rows
    piece = out_ref.shape[1] // members
    core = core_ref[0]
    half = flat // 2
    for side, weighted in enumerate((own_ref, other_ref)):
        part = core if side == 0 else 1 - core
        for t in range(half // SUB):
            at = pl.ds(pl.multiple_of(part * half + t * SUB, SUB), SUB)
            level = part * (levels // 2) + t * (SUB // rows)
            parts = [
                weighted[v * half + t * SUB : v * half + t * SUB + SUB, :]
                for v in range(variables)
            ]
            for k in range(members):
                total = level_pair(perturb_ref, k, 0, level, rows) * parts[0]
                for v in range(1, variables):
                    total = total + level_pair(perturb_ref, k, v, level, rows) * parts[v]
                adjoint[at, LANES * k : LANES * (k + 1)] = total
    whole = dot(band_ref[...], adjoint[...])
    for k in range(members):
        out_ref[:, piece * k : piece * k + piece, :] = whole[
            :, LANES * k : LANES * (k + 1)
        ].reshape(-1, piece, LANES)


def add_up(keep_ref, got_ref, out_ref):
    out_ref[...] = keep_ref[...] + got_ref[...]


def weigh(weight_ref, on_chip_ref, got_ref, out_ref):
    out_ref[...] = weight_ref[...] * (on_chip_ref[...] + got_ref[...])


def call(kernel, out_shape, flops, moved, ins=None, outs=None, scratch=(), limit=8, **grid):
    def run(*args):
        return pl.pallas_call(
            kernel,
            out_shape=out_shape,
            in_specs=ins or [VMEM] * len(args),
            out_specs=outs or jax.tree.map(lambda _: VMEM, out_shape),
            scratch_shapes=scratch,
            cost_estimate=pl.CostEstimate(flops=flops, bytes_accessed=moved, transcendentals=0),
            compiler_params=pltpu.CompilerParams(vmem_limit_bytes=limit << 20),
            **grid,
        )(*args)

    return run


def f32(*shape):
    return jax.ShapeDtypeStruct(shape, jnp.float32)


def local(control, perturb, obs_count, obs_kind, obs_table, band_filter, diffusivity):
    members, level_planes, lat, lon = control.shape
    variables, levels, rows = perturb.shape[1:4]
    devices = lax.axis_size("wide")
    planes = members * level_planes
    steps = lon // SUB
    flat = levels * rows
    half = flat // 2
    chunk = 2
    tiles = -(-lon // (chunk * LANES)) * chunk
    width = chunk * LANES
    height = planes * rows
    control_t = jnp.swapaxes(control, 2, 3).reshape(planes, lon, lat)
    control_t = pltpu.with_memory_space_constraint(control_t, pltpu.HBM)
    diff_t = jnp.swapaxes(diffusivity, 0, 1)
    core = (lax.axis_index("mem") % 2).astype(jnp.int32).reshape(1)

    coefs = f32(rows, steps, SUB, LANES)
    vmem = [
        (planes, lon, lat),
        coefs.shape,
        coefs.shape,
        coefs.shape,
        (tiles, planes * lat, LANES),
        (rows, tiles * LANES, LANES),
    ]
    vmem = [pltpu.VMEM(shape, jnp.float32) for shape in vmem]
    work = planes * lat * lon * ITERS * 8
    size = planes * lat * lon * 4

    sent, east, north = call(
        spread_out,
        [f32(devices * tiles * height, LANES)] + [pltpu.HBM(coefs.shape, coefs.dtype)] * 2,
        work,
        2 * size,
        [HBM, VMEM],
        [VMEM, HBM, HBM],
        [*vmem, pltpu.SemaphoreType.DMA((3,))],
        20,
    )(control_t, diff_t)
    east, north = (pltpu.with_memory_space_constraint(e, pltpu.HBM) for e in (east, north))

    def exchange(sent):
        return lax.all_to_all(sent.reshape(devices, -1, height, LANES), "wide", 0, 0, tiled=True)

    pieces = exchange(sent)

    part = f32(variables * half, width)
    band, band_t, *weights = call(
        prepare,
        [f32(flat, flat), f32(flat, flat)] + [part] * (tiles // chunk),
        1 << 28,
        4 << 20,
        [SMEM] + [VMEM] * 4,
    )(core, band_filter, obs_table, obs_count, obs_kind)

    other_core = [(i, i ^ 1) for i in range(4)]
    next_chip = [(i, i ^ 2) for i in range(4)]
    perturb = pltpu.with_memory_space_constraint(perturb, pltpu.HBM)
    in_band = pl.BlockSpec((flat, flat), lambda g: (0, 0))
    in_part = pl.BlockSpec((variables * half, LANES), lambda g: (0, g))
    scratch = [pltpu.VMEM((flat, members * LANES), jnp.float32)]
    home = None
    lifted = []
    for h in range(tiles // chunk):
        in_piece = pl.BlockSpec(
            (devices, None, height, LANES), lambda g, h=h: (0, h * chunk + g, 0, 0)
        )
        in_perturb = pl.BlockSpec(
            (members, variables, levels, rows, LANES),
            lambda g, h=h: (0, 0, 0, 0, h * chunk + g),
        )
        send, keep = call(
            partial_sums,
            [part, part],
            1 << 29,
            4 * size,
            [SMEM, in_band, in_piece, in_perturb],
            [in_part, in_part],
            scratch,
            grid=(chunk,),
        )(core, band, pieces, perturb)
        got = lax.ppermute(send, "mem", other_core)
        on_chip = call(add_up, part, 1 << 18, size)(keep, got)
        got = lax.ppermute(on_chip, "mem", next_chip)
        own = call(weigh, part, 1 << 18, size)(weights[h], on_chip, got)
        other = lax.ppermute(own, "mem", other_core)
        first, last = h < 2, h != 1
        count = chunk if h == 0 else tiles - chunk
        out_piece = pl.BlockSpec(
            (devices, None, height, LANES), lambda g, h=h: (0, max(h - 1, 0) * chunk + g, 0, 0)
        )
        home = call(
            lift,
            f32(devices, count, height, LANES),
            1 << 29,
            4 * size,
            [SMEM, in_band, in_part, in_part, in_perturb]
            + ([] if first else [pl.BlockSpec(memory_space=pl.ANY)]),
            out_piece,
            scratch,
            grid=(chunk,),
            input_output_aliases={} if first else {5: 0},
        )(core, band_t, own, other, perturb, *([] if first else [home]))
        if last:
            lifted.append(exchange(home).reshape(-1, LANES))

    out = call(
        gather_in,
        pltpu.HBM((planes, lon, lat), jnp.float32),
        work,
        3 * size,
        [VMEM, VMEM, HBM, HBM, HBM],
        HBM,
        [*vmem, pltpu.SemaphoreType.DMA((3 + planes,))],
        20,
    )(*lifted, control_t, east, north)
    return jnp.swapaxes(out.reshape(members, level_planes, lon, lat), 2, 3)


def solution(mesh):
    placed = (
        P("mem", "wide", None, None),
        P("mem", None, None, "wide", None),
        P("wide", None),
        P("wide", None),
        P(),
        P(),
        P(),
    )

    return jax.shard_map(
        local, mesh=mesh, in_specs=placed, out_specs=P("mem", "wide", None, None), check_vma=False
    )
```

```python
import jax
import jax.numpy as jnp
from jax import lax
from jax.experimental import pallas as pl
from jax.experimental.pallas import tpu as pltpu
from jax.sharding import PartitionSpec as P


ITERS = 16
SUB = 8
LANES = 128
VMEM = pl.BlockSpec(memory_space=pltpu.VMEM)
SMEM = pl.BlockSpec(memory_space=pltpu.SMEM)
HBM = pl.BlockSpec(memory_space=pltpu.HBM)
HIGHEST = lax.Precision.HIGHEST


def dot(a, b, contract=((1,), (0,))):
    return lax.dot_general(
        a, b, (contract, ((), ())), precision=HIGHEST, preferred_element_type=jnp.float32
    )


def iota(shape, dim):
    return lax.broadcasted_iota(jnp.int32, shape, dim)


def ones_where(mask):
    return jnp.where(mask, 1.0, 0.0).astype(jnp.float32)


def blocks_of(lon):
    return [(start, min(LANES, lon - start)) for start in range(0, lon, LANES)]


def coefficients(diff_ref, east, north, turned, flat):
    rows, steps = east.shape[:2]
    lon, lat = diff_ref.shape
    blocks = lat // rows
    copies = LANES // blocks
    for start, width in blocks_of(lon):
        turned[start // LANES, :lat, :width] = diff_ref[start : start + width, :].T
    for i in range(rows):
        for start, width in blocks_of(lon):
            picked = turned[start // LANES, pl.ds(i, blocks, stride=rows), :]
            flat[i, start : start + LANES, :] = jnp.concatenate([picked] * copies, 0).T
    edge = lax.rem(iota((SUB, LANES), 1), blocks) == blocks - 1
    first = [flat[i, pl.ds(0, SUB, stride=steps), :] for i in range(rows)]
    here = list(first)
    for r in range(steps):
        for i in range(rows):
            if r + 1 < steps:
                there = flat[i, pl.ds(r + 1, SUB, stride=steps), :]
            else:
                there = pltpu.roll(first[i], SUB - 1, 0)
            east[i, r] = 0.5 * (here[i] + there)
            if i + 1 < rows:
                north[i, r] = 0.5 * (here[i] + here[i + 1])
            else:
                up = 0.5 * (here[i] + pltpu.roll(start_of_row, LANES - 1, 1))
                north[i, r] = jnp.where(edge, jnp.zeros_like(up), up)
            if i == 0:
                start_of_row = here[0]
            here[i] = there if i else here[i]
            if i == 0:
                next_of_row = there
        here[0] = next_of_row


def diffuse_in_place(field, east, north):
    rows, steps = field.shape[:2]

    def one_step(step_index, carry):
        here = [field[i, 0] for i in range(rows)]
        ahead = [pltpu.roll(f, SUB - 1, 0) for f in here]
        before = [
            pltpu.roll(east[i, steps - 1] * (ahead[i] - field[i, steps - 1]), 1, 0)
            for i in range(rows)
        ]
        for r in range(steps):
            there = [field[i, r + 1] if r + 1 < steps else ahead[i] for i in range(rows)]
            up = here[1:] + [pltpu.roll(here[0], LANES - 1, 1)]
            flux_north = [north[i, r] * (up[i] - here[i]) for i in range(rows)]
            down = [pltpu.roll(flux_north[-1], 1, 1)] + flux_north[:-1]
            for i in range(rows):
                flux_east = east[i, r] * (there[i] - here[i])
                field[i, r] = here[i] + ((flux_east - before[i]) + (flux_north[i] - down[i]))
                before[i] = flux_east
            here = there
        return carry

    lax.fori_loop(0, ITERS, one_step, 0)


def spread_out(
    control_hbm, diff_hbm, sent_ref, east_hbm, north_hbm,
    diffusivity, control, east, north, field, turned, flat, sems,
):
    planes, lon, lat = control.shape
    rows, steps = field.shape[:2]
    blocks = lat // rows
    tiles = turned.shape[0]
    fetch_diff = pltpu.make_async_copy(diff_hbm, diffusivity, sems.at[0])
    fetch_diff.start()
    fetch = pltpu.make_async_copy(control_hbm, control, sems.at[1])
    fetch.start()
    turned[tiles - 1] = jnp.zeros(turned.shape[1:], jnp.float32)
    flat[:, (tiles - 1) * LANES :, :] = jnp.zeros((rows, LANES, LANES), jnp.float32)
    fetch_diff.wait()
    coefficients(diffusivity, east, north, turned, flat)
    keep_east = pltpu.make_async_copy(east, east_hbm, sems.at[2])
    keep_north = pltpu.make_async_copy(north, north_hbm, sems.at[3])
    keep_east.start()
    keep_north.start()
    fetch.wait()
    for q in range(planes):
        for start, width in blocks_of(lon):
            turned[start // LANES, lat * q : lat * q + lat, :width] = control[
                q, start : start + width, :
            ].T
    for i in range(rows):
        for start, width in blocks_of(lon):
            picked = [
                turned[start // LANES, pl.ds(lat * q + i, blocks, stride=rows), :]
                for q in range(planes)
            ]
            flat[i, start : start + LANES, :] = jnp.concatenate(picked, 0).T
        for r in range(steps):
            field[i, r] = flat[i, pl.ds(r, SUB, stride=steps), :]
    diffuse_in_place(field, east, north)
    for i in range(rows):
        for r in range(steps):
            flat[i, pl.ds(r, SUB, stride=steps), :] = field[i, r]
        for start, width in blocks_of(lon):
            block = flat[i, start : start + LANES, :].T
            for q in range(planes):
                row = (start // LANES * planes + q) * rows + i
                sent_ref[pl.ds(row, blocks, stride=tiles * planes * rows), :] = block[
                    q * blocks : (q + 1) * blocks, :
                ]
    keep_east.wait()
    keep_north.wait()


def gather_in(
    a_ref, b_ref, control_hbm, east_hbm, north_hbm, out_hbm,
    control, east, north, field, turned, flat, sems,
):
    planes, lon, lat = control.shape
    rows, steps = field.shape[:2]
    blocks = lat // rows
    tiles_a = a_ref.shape[0] // (blocks * planes * rows)
    tiles_b = b_ref.shape[0] // (blocks * planes * rows)
    fetches = [
        pltpu.make_async_copy(source, target, sems.at[planes + n])
        for n, (source, target) in enumerate(
            ((east_hbm, east), (north_hbm, north), (control_hbm, control))
        )
    ]
    for fetch in fetches:
        fetch.start()
    for i in range(rows):
        for start, width in blocks_of(lon):
            in_ref, tile, tiles = a_ref, start // LANES, tiles_a
            if tile >= tiles_a:
                in_ref, tile, tiles = b_ref, tile - tiles_a, tiles_b
            picked = [
                in_ref[
                    pl.ds((tile * planes + q) * rows + i, blocks, stride=tiles * planes * rows), :
                ]
                for q in range(planes)
            ]
            flat[i, start : start + LANES, :] = jnp.concatenate(picked, 0).T
        for r in range(steps):
            field[i, r] = flat[i, pl.ds(r, SUB, stride=steps), :]
    fetches[0].wait()
    fetches[1].wait()
    diffuse_in_place(field, east, north)
    for i in range(rows):
        for r in range(steps):
            flat[i, pl.ds(r, SUB, stride=steps), :] = field[i, r]
        for start, width in blocks_of(lon):
            block = flat[i, start : start + LANES, :].T
            for q in range(planes):
                turned[start // LANES, pl.ds(lat * q + i, blocks, stride=rows), :] = block[
                    q * blocks : (q + 1) * blocks, :
                ]
    fetches[2].wait()
    stores = []
    for q in range(planes):
        for start, width in blocks_of(lon):
            back = turned[start // LANES, lat * q : lat * q + lat, :].T
            place = pl.ds(start, width)
            control[q, place, :] = control[q, place, :] + back[:width, :]
        stores.append(pltpu.make_async_copy(control.at[q], out_hbm.at[q], sems.at[q]))
        stores[-1].start()
    for store in stores:
        store.wait()


def prepare(core_ref, filter_ref, table_ref, count_ref, kind_ref, band_ref, band_t_ref, *weight_refs):
    levels = filter_ref.shape[0]
    flat = band_ref.shape[0]
    rows = flat // levels
    kinds, columns = table_ref.shape
    lon = count_ref.shape[1]
    own = weight_refs[0].shape[0]
    variables = columns // levels
    share = own // variables // rows
    spread = ones_where(iota((flat, levels), 0) // rows == iota((flat, levels), 1))
    spread_t = ones_where(iota((levels, flat), 1) // rows == iota((levels, flat), 0))
    same = lax.rem(iota((flat, flat), 0), rows) == lax.rem(iota((flat, flat), 1), rows)
    weight = filter_ref[...]
    band_ref[...] = jnp.where(same, dot(dot(spread, weight), spread_t), 0.0)
    band_t_ref[...] = jnp.where(same, dot(dot(spread, weight, ((1,), (1,))), spread_t), 0.0)
    row = iota((own, columns), 0)
    column = (
        row // (share * rows) * levels
        + core_ref[0] * share
        + lax.rem(row // rows, share)
    )
    picked = dot(ones_where(column == iota((own, columns), 1)), table_ref[...], ((1,), (1,)))
    wide = kinds * rows
    each = ones_where(iota((kinds, wide), 1) // rows == iota((kinds, wide), 0))
    match = lax.rem(iota((own, wide), 0), rows) == lax.rem(iota((own, wide), 1), rows)
    table = jnp.where(match, dot(picked, each), 0.0)
    repeat = ones_where(lax.rem(iota((wide, rows), 0), rows) == iota((wide, rows), 1))
    kind = dot(repeat, kind_ref[...].astype(jnp.float32))
    count = dot(repeat, count_ref[...].astype(jnp.float32))
    which = (iota((wide, lon), 0) // rows).astype(jnp.float32)
    chosen = jnp.where(kind == which, count, 0.0)
    start = 0
    for weight_ref in weight_refs[:-1]:
        width = weight_ref.shape[1]
        weight_ref[...] = dot(table, chosen[:, start : start + width])
        start += width
    tail = jnp.concatenate(
        [chosen[:, start:], jnp.zeros((wide, start + LANES - lon), jnp.float32)], 1
    )
    weight_refs[-1][...] = dot(table, tail).T[: lon - start, :]


def rows_of(perturb_ref, out_ref):
    levels, rows, lon = perturb_ref.shape
    pair = SUB // rows
    for tile, (start, width) in enumerate(blocks_of(lon)):
        if width < LANES:
            out_ref[tile] = jnp.zeros(out_ref.shape[1:], jnp.float32)
        for t in range(levels // pair):
            out_ref[tile, SUB * t : SUB * t + SUB, :width] = jnp.concatenate(
                [perturb_ref[pair * t + u, :, start : start + width] for u in range(pair)], 0
            )


def partial_sums(core_ref, band_ref, pieces_ref, perturb_ref, send_ref, keep_ref, filtered, parts):
    members, flat = filtered.shape[1] // LANES, perturb_ref.shape[1]
    variables = perturb_ref.shape[0] // members
    piece = pieces_ref.shape[1] // members
    core = core_ref[0]
    half = flat // 2
    mine = [
        pieces_ref[:, piece * k : piece * k + piece, :].reshape(flat, LANES)
        for k in range(members)
    ]
    filtered[...] = dot(band_ref[...], jnp.concatenate(mine, 1))
    for side, out_ref in enumerate((send_ref, keep_ref)):
        base = (core if side else 1 - core) * half
        turned = out_ref.shape[0] < variables * half
        to_ref = parts.at[side] if turned else out_ref
        for t in range(half // SUB):
            at = pl.ds(pl.multiple_of(base + t * SUB, SUB), SUB)
            fields = [filtered[at, LANES * k : LANES * (k + 1)] for k in range(members)]
            for v in range(variables):
                total = perturb_ref[v, at, :] * fields[0]
                for k in range(1, members):
                    total = total + perturb_ref[k * variables + v, at, :] * fields[k]
                row = v * half + t * SUB
                to_ref[row : row + SUB, :] = total
        if turned:
            for v in range(variables):
                block = parts[side, v * half : (v + 1) * half, :].T
                out_ref[:, v * half : (v + 1) * half] = block[: out_ref.shape[0], :]


def lift(core_ref, band_ref, own_ref, other_ref, perturb_ref, *rest):
    out_ref, adjoint, parts = rest[-3:]
    members, flat = adjoint.shape[1] // LANES, perturb_ref.shape[1]
    variables = perturb_ref.shape[0] // members
    piece = out_ref.shape[1] // members
    core = core_ref[0]
    half = flat // 2
    sides = [own_ref, other_ref]
    if own_ref.shape[0] < variables * half:
        empty = jnp.zeros((LANES - own_ref.shape[0], half), jnp.float32)
        for side, weighted in enumerate(sides):
            for v in range(variables):
                block = jnp.concatenate([weighted[:, v * half : (v + 1) * half], empty], 0)
                parts[side, v * half : (v + 1) * half, :] = block.T
        sides = [parts.at[0], parts.at[1]]
    for side, weighted in enumerate(sides):
        base = (core if side == 0 else 1 - core) * half
        for t in range(half // SUB):
            at = pl.ds(pl.multiple_of(base + t * SUB, SUB), SUB)
            terms = [
                weighted[v * half + t * SUB : v * half + t * SUB + SUB, :]
                for v in range(variables)
            ]
            for k in range(members):
                total = perturb_ref[k * variables, at, :] * terms[0]
                for v in range(1, variables):
                    total = total + perturb_ref[k * variables + v, at, :] * terms[v]
                adjoint[at, LANES * k : LANES * (k + 1)] = total
    whole = dot(band_ref[...], adjoint[...])
    for k in range(members):
        out_ref[:, piece * k : piece * k + piece, :] = whole[
            :, LANES * k : LANES * (k + 1)
        ].reshape(-1, piece, LANES)


def add_up(keep_ref, got_ref, out_ref):
    out_ref[...] = keep_ref[...] + got_ref[...]


def weigh(weight_ref, on_chip_ref, got_ref, out_ref):
    out_ref[...] = weight_ref[...] * (on_chip_ref[...] + got_ref[...])


def call(kernel, out_shape, flops, moved, ins=None, outs=None, scratch=(), limit=8, **grid):
    def run(*args):
        return pl.pallas_call(
            kernel,
            out_shape=out_shape,
            in_specs=ins or [VMEM] * len(args),
            out_specs=outs or jax.tree.map(lambda _: VMEM, out_shape),
            scratch_shapes=scratch,
            cost_estimate=pl.CostEstimate(flops=flops, bytes_accessed=moved, transcendentals=0),
            compiler_params=pltpu.CompilerParams(vmem_limit_bytes=limit << 20),
            **grid,
        )(*args)

    return run


def f32(*shape):
    return jax.ShapeDtypeStruct(shape, jnp.float32)


def local(control, perturb, obs_count, obs_kind, obs_table, band_filter, diffusivity):
    members, level_planes, lat, lon = control.shape
    variables, levels, rows = perturb.shape[1:4]
    devices = lax.axis_size("wide")
    planes = members * level_planes
    steps = lon // SUB
    flat = levels * rows
    half = flat // 2
    tiles = -(-lon // LANES)
    chunks = [(0, 1), (1, 1), (2, tiles - 3), (tiles - 1, 1)]
    groups = {0: (0, 2), 1: (0, 2), 2: (2, tiles - 2), 3: (2, tiles - 2)}
    height = planes * rows
    control_t = jnp.swapaxes(control, 2, 3).reshape(planes, lon, lat)
    control_t = pltpu.with_memory_space_constraint(control_t, pltpu.HBM)
    diff_t = jnp.swapaxes(diffusivity, 0, 1)
    core = (lax.axis_index("mem") % 2).astype(jnp.int32).reshape(1)

    coefs = f32(rows, steps, SUB, LANES)
    vmem = [
        (planes, lon, lat),
        coefs.shape,
        coefs.shape,
        coefs.shape,
        (tiles, planes * lat, LANES),
        (rows, tiles * LANES, LANES),
    ]
    vmem = [pltpu.VMEM(shape, jnp.float32) for shape in vmem]
    resting = pltpu.HBM(coefs.shape, jnp.float32)
    work = planes * lat * lon * ITERS * 8
    size = planes * lat * lon * 4

    sent, east, north = call(
        spread_out,
        [f32(devices * tiles * height, LANES), resting, resting],
        work,
        2 * size,
        [HBM, HBM],
        [VMEM, HBM, HBM],
        [pltpu.VMEM((lon, lat), jnp.float32), *vmem, pltpu.SemaphoreType.DMA((4,))],
        20,
    )(control_t, pltpu.with_memory_space_constraint(diff_t, pltpu.HBM))
    east, north = (pltpu.with_memory_space_constraint(e, pltpu.HBM) for e in (east, north))

    def exchange(sent):
        return lax.all_to_all(sent.reshape(devices, -1, height, LANES), "wide", 0, 0, tiled=True)

    pieces = exchange(sent)

    used = lon - (tiles - 1) * LANES
    parts = [f32(variables * half, count * LANES) for first, count in chunks[:-1]]
    parts.append(f32(used, variables * half))
    band, band_t, *weights = call(
        prepare,
        [f32(flat, flat), f32(flat, flat)] + parts,
        1 << 28,
        4 << 20,
        [SMEM] + [VMEM] * 4,
    )(core, band_filter, obs_table, obs_count, obs_kind)
    perturb = perturb.reshape(members * variables, levels, rows, lon)
    perturb = call(
        rows_of,
        f32(tiles, members * variables, flat, LANES),
        1 << 20,
        6 * size,
        [pl.BlockSpec((None, levels, rows, lon), lambda g: (g, 0, 0, 0))],
        pl.BlockSpec((tiles, None, flat, LANES), lambda g: (0, g, 0, 0)),
        grid=(members * variables,),
    )(pltpu.with_memory_space_constraint(perturb, pltpu.HBM))
    perturb = pltpu.with_memory_space_constraint(perturb, pltpu.HBM)

    other_core = [(i, i ^ 1) for i in range(4)]
    next_chip = [(i, i ^ 2) for i in range(4)]
    home = None
    lifted = []
    for h, (first, count) in enumerate(chunks):
        part = parts[h]
        scratch = [
            pltpu.VMEM((flat, members * LANES), jnp.float32),
            pltpu.VMEM((2, variables * half, LANES), jnp.float32),
        ]
        in_band = pl.BlockSpec((flat, flat), lambda g: (0, 0))
        in_part = pl.BlockSpec((part.shape[0], part.shape[1] // count), lambda g: (0, g))
        in_perturb = pl.BlockSpec(
            (None, members * variables, flat, LANES), lambda g, first=first: (first + g, 0, 0, 0)
        )

        def piece_at(first):
            return pl.BlockSpec(
                (devices, None, height, LANES), lambda g, first=first: (0, first + g, 0, 0)
            )

        send, keep = call(
            partial_sums,
            [part, part],
            count << 28,
            count * size,
            [SMEM, in_band, piece_at(first), in_perturb],
            [in_part, in_part],
            scratch,
            grid=(count,),
        )(core, band, pieces, perturb)
        got = lax.ppermute(send, "mem", other_core)
        on_chip = call(add_up, part, 1 << 18, size)(keep, got)
        got = lax.ppermute(on_chip, "mem", next_chip)
        own = call(weigh, part, 1 << 18, size)(weights[h], on_chip, got)
        other = lax.ppermute(own, "mem", other_core)
        start, total = groups[h]
        begins = first == start

        home = call(
            lift,
            f32(devices, total, height, LANES),
            count << 28,
            count * size,
            [SMEM, in_band, in_part, in_part, in_perturb]
            + ([] if begins else [pl.BlockSpec(memory_space=pl.ANY)]),
            piece_at(first - start),
            scratch,
            grid=(count,),
            input_output_aliases={} if begins else {5: 0},
        )(core, band_t, own, other, perturb, *([] if begins else [home]))
        if first + count == start + total:
            lifted.append(exchange(home).reshape(-1, LANES))

    out = call(
        gather_in,
        pltpu.HBM((planes, lon, lat), jnp.float32),
        work,
        3 * size,
        [VMEM, VMEM, HBM, HBM, HBM],
        HBM,
        [*vmem, pltpu.SemaphoreType.DMA((planes + 3,))],
        20,
    )(*lifted, control_t, east, north)
    return jnp.swapaxes(out.reshape(members, level_planes, lon, lat), 2, 3)


def solution(mesh):
    placed = (
        P("mem", "wide", None, None),
        P("mem", None, None, "wide", None),
        P("wide", None),
        P("wide", None),
        P(),
        P(),
        P(),
    )

    return jax.shard_map(
        local, mesh=mesh, in_specs=placed, out_specs=P("mem", "wide", None, None), check_vma=False
    )
```

```python
import functools

import jax
import jax.numpy as jnp
from jax import lax
from jax.experimental import pallas as pl
from jax.experimental.pallas import tpu as pltpu
from jax.sharding import PartitionSpec as P


ITERS = 16
SUB = 8
LANES = 128
VMEM = pl.BlockSpec(memory_space=pltpu.VMEM)
SMEM = pl.BlockSpec(memory_space=pltpu.SMEM)
HBM = pl.BlockSpec(memory_space=pltpu.HBM)
HIGHEST = lax.Precision.HIGHEST


def dot(a, b, contract=((1,), (0,))):
    return lax.dot_general(
        a, b, (contract, ((), ())), precision=HIGHEST, preferred_element_type=jnp.float32
    )


def iota(shape, dim):
    return lax.broadcasted_iota(jnp.int32, shape, dim)


def ones_where(mask):
    return jnp.where(mask, 1.0, 0.0).astype(jnp.float32)


def blocks_of(lon):
    return [(start, min(LANES, lon - start)) for start in range(0, lon, LANES)]


def coefficients(diff_ref, east, north, turned, flat):
    rows, steps = east.shape[:2]
    lon, lat = diff_ref.shape
    blocks = lat // rows
    copies = LANES // blocks
    for start, width in blocks_of(lon):
        turned[start // LANES, :lat, :width] = diff_ref[start : start + width, :].T
    for i in range(rows):
        for start, width in blocks_of(lon):
            picked = turned[start // LANES, pl.ds(i, blocks, stride=rows), :]
            flat[i, start : start + LANES, :] = jnp.concatenate([picked] * copies, 0).T
    edge = lax.rem(iota((SUB, LANES), 1), blocks) == blocks - 1
    first = [flat[i, pl.ds(0, SUB, stride=steps), :] for i in range(rows)]
    here = list(first)
    for r in range(steps):
        for i in range(rows):
            if r + 1 < steps:
                there = flat[i, pl.ds(r + 1, SUB, stride=steps), :]
            else:
                there = pltpu.roll(first[i], SUB - 1, 0)
            east[i, r] = 0.5 * (here[i] + there)
            if i + 1 < rows:
                north[i, r] = 0.5 * (here[i] + here[i + 1])
            else:
                up = 0.5 * (here[i] + pltpu.roll(start_of_row, LANES - 1, 1))
                north[i, r] = jnp.where(edge, jnp.zeros_like(up), up)
            if i == 0:
                start_of_row = here[0]
            here[i] = there if i else here[i]
            if i == 0:
                next_of_row = there
        here[0] = next_of_row


def diffuse_in_place(field, east, north):
    rows, steps = field.shape[:2]

    def one_step(step_index, carry):
        here = [field[i, 0] for i in range(rows)]
        ahead = [pltpu.roll(f, SUB - 1, 0) for f in here]
        before = [
            pltpu.roll(east[i, steps - 1] * (ahead[i] - field[i, steps - 1]), 1, 0)
            for i in range(rows)
        ]
        for r in range(steps):
            there = [field[i, r + 1] if r + 1 < steps else ahead[i] for i in range(rows)]
            up = here[1:] + [pltpu.roll(here[0], LANES - 1, 1)]
            flux_north = [north[i, r] * (up[i] - here[i]) for i in range(rows)]
            down = [pltpu.roll(flux_north[-1], 1, 1)] + flux_north[:-1]
            for i in range(rows):
                flux_east = east[i, r] * (there[i] - here[i])
                field[i, r] = here[i] + ((flux_east - before[i]) + (flux_north[i] - down[i]))
                before[i] = flux_east
            here = there
        return carry

    lax.fori_loop(0, ITERS, one_step, 0)


def spread_out(
    control_hbm, diff_hbm, sent_ref, east_hbm, north_hbm,
    diffusivity, control, east, north, field, turned, flat, sems,
):
    planes, lon, lat = control.shape
    rows, steps = field.shape[:2]
    blocks = lat // rows
    tiles = turned.shape[0]
    fetch_diff = pltpu.make_async_copy(diff_hbm, diffusivity, sems.at[0])
    fetch_diff.start()
    fetch = pltpu.make_async_copy(control_hbm, control, sems.at[1])
    fetch.start()
    turned[tiles - 1] = jnp.zeros(turned.shape[1:], jnp.float32)
    flat[:, (tiles - 1) * LANES :, :] = jnp.zeros((rows, LANES, LANES), jnp.float32)
    fetch_diff.wait()
    coefficients(diffusivity, east, north, turned, flat)
    keep_east = pltpu.make_async_copy(east, east_hbm, sems.at[2])
    keep_north = pltpu.make_async_copy(north, north_hbm, sems.at[3])
    keep_east.start()
    keep_north.start()
    fetch.wait()
    for q in range(planes):
        for start, width in blocks_of(lon):
            turned[start // LANES, lat * q : lat * q + lat, :width] = control[
                q, start : start + width, :
            ].T
    for i in range(rows):
        for start, width in blocks_of(lon):
            picked = [
                turned[start // LANES, pl.ds(lat * q + i, blocks, stride=rows), :]
                for q in range(planes)
            ]
            flat[i, start : start + LANES, :] = jnp.concatenate(picked, 0).T
        for r in range(steps):
            field[i, r] = flat[i, pl.ds(r, SUB, stride=steps), :]
    diffuse_in_place(field, east, north)
    for i in range(rows):
        for r in range(steps):
            flat[i, pl.ds(r, SUB, stride=steps), :] = field[i, r]
        for start, width in blocks_of(lon):
            block = flat[i, start : start + LANES, :].T
            for q in range(planes):
                row = (start // LANES * planes + q) * rows + i
                sent_ref[pl.ds(row, blocks, stride=tiles * planes * rows), :] = block[
                    q * blocks : (q + 1) * blocks, :
                ]
    keep_east.wait()
    keep_north.wait()


def gather_in(
    a_ref, b_ref, control_hbm, east_hbm, north_hbm, out_hbm,
    control, east, north, field, turned, flat, sems,
):
    planes, lon, lat = control.shape
    rows, steps = field.shape[:2]
    blocks = lat // rows
    tiles_a = a_ref.shape[0] // (blocks * planes * rows)
    tiles_b = b_ref.shape[0] // (blocks * planes * rows)
    fetches = [
        pltpu.make_async_copy(source, target, sems.at[planes + n])
        for n, (source, target) in enumerate(
            ((east_hbm, east), (north_hbm, north), (control_hbm, control))
        )
    ]
    for fetch in fetches:
        fetch.start()
    for i in range(rows):
        for start, width in blocks_of(lon):
            in_ref, tile, tiles = a_ref, start // LANES, tiles_a
            if tile >= tiles_a:
                in_ref, tile, tiles = b_ref, tile - tiles_a, tiles_b
            picked = [
                in_ref[
                    pl.ds((tile * planes + q) * rows + i, blocks, stride=tiles * planes * rows), :
                ]
                for q in range(planes)
            ]
            flat[i, start : start + LANES, :] = jnp.concatenate(picked, 0).T
        for r in range(steps):
            field[i, r] = flat[i, pl.ds(r, SUB, stride=steps), :]
    fetches[0].wait()
    fetches[1].wait()
    diffuse_in_place(field, east, north)
    for i in range(rows):
        for r in range(steps):
            flat[i, pl.ds(r, SUB, stride=steps), :] = field[i, r]
        for start, width in blocks_of(lon):
            block = flat[i, start : start + LANES, :].T
            for q in range(planes):
                turned[start // LANES, pl.ds(lat * q + i, blocks, stride=rows), :] = block[
                    q * blocks : (q + 1) * blocks, :
                ]
    fetches[2].wait()
    stores = []
    for q in range(planes):
        for start, width in blocks_of(lon):
            back = turned[start // LANES, lat * q : lat * q + lat, :].T
            place = pl.ds(start, width)
            control[q, place, :] = control[q, place, :] + back[:width, :]
        stores.append(pltpu.make_async_copy(control.at[q], out_hbm.at[q], sems.at[q]))
        stores[-1].start()
    for store in stores:
        store.wait()


def prepare(core_ref, filter_ref, table_ref, count_ref, kind_ref, band_ref, band_t_ref, *weight_refs):
    levels = filter_ref.shape[0]
    flat = band_ref.shape[0]
    rows = flat // levels
    kinds, columns = table_ref.shape
    lon = count_ref.shape[1]
    own = weight_refs[0].shape[0]
    variables = columns // levels
    share = own // variables // rows
    spread = ones_where(iota((flat, levels), 0) // rows == iota((flat, levels), 1))
    spread_t = ones_where(iota((levels, flat), 1) // rows == iota((levels, flat), 0))
    same = lax.rem(iota((flat, flat), 0), rows) == lax.rem(iota((flat, flat), 1), rows)
    weight = filter_ref[...]
    band_ref[...] = jnp.where(same, dot(dot(spread, weight), spread_t), 0.0)
    band_t_ref[...] = jnp.where(same, dot(dot(spread, weight, ((1,), (1,))), spread_t), 0.0)
    row = iota((own, columns), 0)
    column = (
        row // (share * rows) * levels
        + core_ref[0] * share
        + lax.rem(row // rows, share)
    )
    picked = dot(ones_where(column == iota((own, columns), 1)), table_ref[...], ((1,), (1,)))
    wide = kinds * rows
    each = ones_where(iota((kinds, wide), 1) // rows == iota((kinds, wide), 0))
    match = lax.rem(iota((own, wide), 0), rows) == lax.rem(iota((own, wide), 1), rows)
    table = jnp.where(match, dot(picked, each), 0.0)
    repeat = ones_where(lax.rem(iota((wide, rows), 0), rows) == iota((wide, rows), 1))
    kind = dot(repeat, kind_ref[...].astype(jnp.float32))
    count = dot(repeat, count_ref[...].astype(jnp.float32))
    which = (iota((wide, lon), 0) // rows).astype(jnp.float32)
    chosen = jnp.where(kind == which, count, 0.0)
    start = 0
    for weight_ref in weight_refs[:-1]:
        width = weight_ref.shape[1]
        weight_ref[...] = dot(table, chosen[:, start : start + width])
        start += width
    tail = jnp.concatenate(
        [chosen[:, start:], jnp.zeros((wide, start + LANES - lon), jnp.float32)], 1
    )
    weight_refs[-1][...] = dot(table, tail).T[: lon - start, :]


def rows_of(perturb_ref, out_ref):
    levels, rows, lon = perturb_ref.shape
    pair = SUB // rows
    for tile, (start, width) in enumerate(blocks_of(lon)):
        if width < LANES:
            out_ref[tile] = jnp.zeros(out_ref.shape[1:], jnp.float32)
        for t in range(levels // pair):
            out_ref[tile, SUB * t : SUB * t + SUB, :width] = jnp.concatenate(
                [perturb_ref[pair * t + u, :, start : start + width] for u in range(pair)], 0
            )


def fetch_tiles(first, perturb_hbm, perturb, sems):
    copies = [
        pltpu.make_async_copy(perturb_hbm.at[first + u], perturb.at[u], sems.at[u])
        for u in range(perturb.shape[0])
    ]
    for copy in copies:
        copy.start()
    return copies


def partial_sums(
    first, core_ref, band_ref, pieces_ref, perturb_hbm, send_ref, keep_ref,
    perturb, filtered, parts, sems,
):
    count, products, flat = perturb.shape[:3]
    members = filtered.shape[1] // LANES
    variables = products // members
    piece = pieces_ref.shape[2] // members
    core = core_ref[0]
    half = flat // 2
    copies = fetch_tiles(first, perturb_hbm, perturb, sems)
    for u in range(count):
        mine = [
            pieces_ref[:, first + u, piece * k : piece * k + piece, :].reshape(flat, LANES)
            for k in range(members)
        ]
        filtered[...] = dot(band_ref[...], jnp.concatenate(mine, 1))
        copies[u].wait()
        for side, out_ref in enumerate((send_ref, keep_ref)):
            base = (core if side else 1 - core) * half
            turned = out_ref.shape[0] < variables * half
            to_ref = parts.at[side] if turned else out_ref
            for t in range(half // SUB):
                at = pl.ds(pl.multiple_of(base + t * SUB, SUB), SUB)
                fields = [filtered[at, LANES * k : LANES * (k + 1)] for k in range(members)]
                for v in range(variables):
                    total = perturb[u, v, at, :] * fields[0]
                    for k in range(1, members):
                        total = total + perturb[u, k * variables + v, at, :] * fields[k]
                    row = v * half + t * SUB
                    to_ref[row : row + SUB, u * LANES : (u + 1) * LANES] = total
            if turned:
                for v in range(variables):
                    block = parts[side, v * half : (v + 1) * half, :].T
                    out_ref[:, v * half : (v + 1) * half] = block[: out_ref.shape[0], :]


def lift(first, place, core_ref, band_ref, own_ref, other_ref, perturb_hbm, *rest):
    out_ref, perturb, adjoint, parts, sems = rest[-5:]
    count, products, flat = perturb.shape[:3]
    members = adjoint.shape[1] // LANES
    variables = products // members
    piece = out_ref.shape[2] // members
    core = core_ref[0]
    half = flat // 2
    copies = fetch_tiles(first, perturb_hbm, perturb, sems)
    for earlier_ref in rest[:-5]:
        out_ref[:, :place] = earlier_ref[...]
    sides = [own_ref, other_ref]
    if own_ref.shape[0] < variables * half:
        empty = jnp.zeros((LANES - own_ref.shape[0], half), jnp.float32)
        for side, weighted in enumerate(sides):
            for v in range(variables):
                block = jnp.concatenate([weighted[:, v * half : (v + 1) * half], empty], 0)
                parts[side, v * half : (v + 1) * half, :] = block.T
        sides = [parts.at[0], parts.at[1]]
    for u in range(count):
        copies[u].wait()
        for side, weighted in enumerate(sides):
            base = (core if side == 0 else 1 - core) * half
            for t in range(half // SUB):
                at = pl.ds(pl.multiple_of(base + t * SUB, SUB), SUB)
                terms = []
                for v in range(variables):
                    row = v * half + t * SUB
                    terms.append(weighted[row : row + SUB, u * LANES : (u + 1) * LANES])
                for k in range(members):
                    total = perturb[u, k * variables, at, :] * terms[0]
                    for v in range(1, variables):
                        total = total + perturb[u, k * variables + v, at, :] * terms[v]
                    adjoint[at, LANES * k : LANES * (k + 1)] = total
        whole = dot(band_ref[...], adjoint[...])
        for k in range(members):
            out_ref[:, place + u, piece * k : piece * k + piece, :] = whole[
                :, LANES * k : LANES * (k + 1)
            ].reshape(-1, piece, LANES)


def add_up(keep_ref, got_ref, out_ref):
    out_ref[...] = keep_ref[...] + got_ref[...]


def weigh(weight_ref, on_chip_ref, got_ref, out_ref):
    out_ref[...] = weight_ref[...] * (on_chip_ref[...] + got_ref[...])


def call(kernel, out_shape, flops, moved, ins=None, outs=None, scratch=(), limit=8, **grid):
    def run(*args):
        return pl.pallas_call(
            kernel,
            out_shape=out_shape,
            in_specs=ins or [VMEM] * len(args),
            out_specs=outs or jax.tree.map(lambda _: VMEM, out_shape),
            scratch_shapes=scratch,
            cost_estimate=pl.CostEstimate(flops=flops, bytes_accessed=moved, transcendentals=0),
            compiler_params=pltpu.CompilerParams(vmem_limit_bytes=limit << 20),
            **grid,
        )(*args)

    return run


def f32(*shape):
    return jax.ShapeDtypeStruct(shape, jnp.float32)


def local(control, perturb, obs_count, obs_kind, obs_table, band_filter, diffusivity):
    members, level_planes, lat, lon = control.shape
    variables, levels, rows = perturb.shape[1:4]
    devices = lax.axis_size("wide")
    planes = members * level_planes
    steps = lon // SUB
    flat = levels * rows
    half = flat // 2
    tiles = -(-lon // LANES)
    chunks = [(0, 2), (2, tiles - 3), (tiles - 1, 1)]
    groups = [(0, 2), (2, tiles - 2), (2, tiles - 2)]
    height = planes * rows
    control_t = jnp.swapaxes(control, 2, 3).reshape(planes, lon, lat)
    control_t = pltpu.with_memory_space_constraint(control_t, pltpu.HBM)
    diff_t = jnp.swapaxes(diffusivity, 0, 1)
    core = (lax.axis_index("mem") % 2).astype(jnp.int32).reshape(1)

    coefs = f32(rows, steps, SUB, LANES)
    vmem = [
        (planes, lon, lat),
        coefs.shape,
        coefs.shape,
        coefs.shape,
        (tiles, planes * lat, LANES),
        (rows, tiles * LANES, LANES),
    ]
    vmem = [pltpu.VMEM(shape, jnp.float32) for shape in vmem]
    resting = pltpu.HBM(coefs.shape, jnp.float32)
    work = planes * lat * lon * ITERS * 8
    size = planes * lat * lon * 4

    sent, east, north = call(
        spread_out,
        [f32(devices * tiles * height, LANES), resting, resting],
        work,
        2 * size,
        [HBM, HBM],
        [VMEM, HBM, HBM],
        [pltpu.VMEM((lon, lat), jnp.float32), *vmem, pltpu.SemaphoreType.DMA((4,))],
        20,
    )(control_t, pltpu.with_memory_space_constraint(diff_t, pltpu.HBM))
    east, north = (pltpu.with_memory_space_constraint(e, pltpu.HBM) for e in (east, north))

    def exchange(sent):
        return lax.all_to_all(sent.reshape(devices, -1, height, LANES), "wide", 0, 0, tiled=True)

    pieces = exchange(sent)

    used = lon - (tiles - 1) * LANES
    parts = [f32(variables * half, count * LANES) for first, count in chunks[:-1]]
    parts.append(f32(used, variables * half))
    band, band_t, *weights = call(
        prepare,
        [f32(flat, flat), f32(flat, flat)] + parts,
        1 << 28,
        4 << 20,
        [SMEM] + [VMEM] * 4,
    )(core, band_filter, obs_table, obs_count, obs_kind)
    perturb = perturb.reshape(members * variables, levels, rows, lon)
    perturb = call(
        rows_of,
        f32(tiles, members * variables, flat, LANES),
        1 << 20,
        6 * size,
        [pl.BlockSpec((None, levels, rows, lon), lambda g: (g, 0, 0, 0))],
        pl.BlockSpec((tiles, None, flat, LANES), lambda g: (0, g, 0, 0)),
        grid=(members * variables,),
    )(pltpu.with_memory_space_constraint(perturb, pltpu.HBM))
    perturb = pltpu.with_memory_space_constraint(perturb, pltpu.HBM)

    other_core = [(i, i ^ 1) for i in range(4)]
    next_chip = [(i, i ^ 2) for i in range(4)]
    home = None
    lifted = []
    for h, (first, count) in enumerate(chunks):
        part = parts[h]
        scratch = [
            pltpu.VMEM((count, members * variables, flat, LANES), jnp.float32),
            pltpu.VMEM((flat, members * LANES), jnp.float32),
            pltpu.VMEM((2, variables * half, LANES), jnp.float32),
            pltpu.SemaphoreType.DMA((count,)),
        ]
        send, keep = call(
            functools.partial(partial_sums, first),
            [part, part],
            count << 28,
            count * size,
            [SMEM, VMEM, VMEM, HBM],
            None,
            scratch,
        )(core, band, pieces, perturb)
        got = lax.ppermute(send, "mem", other_core)
        on_chip = call(add_up, part, 1 << 18, size)(keep, got)
        got = lax.ppermute(on_chip, "mem", next_chip)
        own = call(weigh, part, 1 << 18, size)(weights[h], on_chip, got)
        other = lax.ppermute(own, "mem", other_core)
        start, total = groups[h]
        place = first - start
        begins = place == 0

        home = call(
            functools.partial(lift, first, place),
            f32(devices, place + count, height, LANES),
            count << 28,
            count * size,
            [SMEM, VMEM, VMEM, VMEM, HBM] + ([] if begins else [VMEM]),
            None,
            scratch,
        )(core, band_t, own, other, perturb, *([] if begins else [home]))
        if first + count == start + total:
            lifted.append(exchange(home).reshape(-1, LANES))

    out = call(
        gather_in,
        pltpu.HBM((planes, lon, lat), jnp.float32),
        work,
        3 * size,
        [VMEM, VMEM, HBM, HBM, HBM],
        HBM,
        [*vmem, pltpu.SemaphoreType.DMA((planes + 3,))],
        20,
    )(*lifted, control_t, east, north)
    return jnp.swapaxes(out.reshape(members, level_planes, lon, lat), 2, 3)


def solution(mesh):
    placed = (
        P("mem", "wide", None, None),
        P("mem", None, None, "wide", None),
        P("wide", None),
        P("wide", None),
        P(),
        P(),
        P(),
    )

    return jax.shard_map(
        local, mesh=mesh, in_specs=placed, out_specs=P("mem", "wide", None, None), check_vma=False
    )
```

```python
import functools

import jax
import jax.numpy as jnp
from jax import lax
from jax.experimental import pallas as pl
from jax.experimental.pallas import tpu as pltpu
from jax.sharding import PartitionSpec as P


ITERS = 16
UNROLL = 4
SUB = 8
LANES = 128
VMEM = pl.BlockSpec(memory_space=pltpu.VMEM)
SMEM = pl.BlockSpec(memory_space=pltpu.SMEM)
HBM = pl.BlockSpec(memory_space=pltpu.HBM)
HIGHEST = lax.Precision.HIGHEST


def dot(a, b, contract=((1,), (0,))):
    return lax.dot_general(
        a, b, (contract, ((), ())), precision=HIGHEST, preferred_element_type=jnp.float32
    )


def iota(shape, dim):
    return lax.broadcasted_iota(jnp.int32, shape, dim)


def ones_where(mask):
    return jnp.where(mask, 1.0, 0.0).astype(jnp.float32)


def blocks_of(lon):
    return [(start, min(LANES, lon - start)) for start in range(0, lon, LANES)]


def coefficients(diff_ref, east, north, turned, flat):
    rows, steps = east.shape[:2]
    lon, lat = diff_ref.shape
    blocks = lat // rows
    copies = LANES // blocks
    for start, width in blocks_of(lon):
        turned[start // LANES, :lat, :width] = diff_ref[start : start + width, :].T
    for i in range(rows):
        for start, width in blocks_of(lon):
            picked = turned[start // LANES, pl.ds(i, blocks, stride=rows), :]
            flat[i, start : start + LANES, :] = jnp.concatenate([picked] * copies, 0).T
    edge = lax.rem(iota((SUB, LANES), 1), blocks) == blocks - 1
    first = [flat[i, pl.ds(0, SUB, stride=steps), :] for i in range(rows)]
    here = list(first)
    for r in range(steps):
        for i in range(rows):
            if r + 1 < steps:
                there = flat[i, pl.ds(r + 1, SUB, stride=steps), :]
            else:
                there = pltpu.roll(first[i], SUB - 1, 0)
            east[i, r] = 0.5 * (here[i] + there)
            if i + 1 < rows:
                north[i, r] = 0.5 * (here[i] + here[i + 1])
            else:
                up = 0.5 * (here[i] + pltpu.roll(start_of_row, LANES - 1, 1))
                north[i, r] = jnp.where(edge, jnp.zeros_like(up), up)
            if i == 0:
                start_of_row = here[0]
            here[i] = there if i else here[i]
            if i == 0:
                next_of_row = there
        here[0] = next_of_row


def diffuse_in_place(field, east, north):
    rows, steps = field.shape[:2]

    def one_step(step_index, carry):
        here = [field[i, 0] for i in range(rows)]
        ahead = [pltpu.roll(f, SUB - 1, 0) for f in here]
        before = [
            pltpu.roll(east[i, steps - 1] * (ahead[i] - field[i, steps - 1]), 1, 0)
            for i in range(rows)
        ]
        for r in range(steps):
            there = [field[i, r + 1] if r + 1 < steps else ahead[i] for i in range(rows)]
            up = here[1:] + [pltpu.roll(here[0], LANES - 1, 1)]
            flux_north = [north[i, r] * (up[i] - here[i]) for i in range(rows)]
            down = [pltpu.roll(flux_north[-1], 1, 1)] + flux_north[:-1]
            for i in range(rows):
                flux_east = east[i, r] * (there[i] - here[i])
                field[i, r] = here[i] + ((flux_east - before[i]) + (flux_north[i] - down[i]))
                before[i] = flux_east
            here = there
        return carry

    lax.fori_loop(0, ITERS, one_step, 0, unroll=UNROLL)


def spread_out(
    control_hbm, diff_hbm, sent_ref, east_hbm, north_hbm,
    diffusivity, control, east, north, field, turned, flat, staged, sems,
):
    planes, lon, lat = control.shape
    rows, steps = field.shape[:2]
    blocks = lat // rows
    tiles = turned.shape[0]
    height = tiles * planes * rows
    pitch = staged.shape[0] // blocks
    fetch_diff = pltpu.make_async_copy(diff_hbm, diffusivity, sems.at[0])
    fetch_diff.start()
    fetch = pltpu.make_async_copy(control_hbm, control, sems.at[1])
    fetch.start()
    turned[tiles - 1] = jnp.zeros(turned.shape[1:], jnp.float32)
    flat[:, (tiles - 1) * LANES :, :] = jnp.zeros((rows, LANES, LANES), jnp.float32)
    fetch_diff.wait()
    coefficients(diffusivity, east, north, turned, flat)
    keep_east = pltpu.make_async_copy(east, east_hbm, sems.at[2])
    keep_north = pltpu.make_async_copy(north, north_hbm, sems.at[3])
    keep_east.start()
    keep_north.start()
    fetch.wait()
    for q in range(planes):
        for start, width in blocks_of(lon):
            turned[start // LANES, lat * q : lat * q + lat, :width] = control[
                q, start : start + width, :
            ].T
    for i in range(rows):
        for start, width in blocks_of(lon):
            picked = [
                turned[start // LANES, pl.ds(lat * q + i, blocks, stride=rows), :]
                for q in range(planes)
            ]
            flat[i, start : start + LANES, :] = jnp.concatenate(picked, 0).T
        for r in range(steps):
            field[i, r] = flat[i, pl.ds(r, SUB, stride=steps), :]
    diffuse_in_place(field, east, north)
    for i in range(rows):
        for r in range(steps):
            flat[i, pl.ds(r, SUB, stride=steps), :] = field[i, r]
        for start, width in blocks_of(lon):
            block = flat[i, start : start + LANES, :].T
            for q in range(planes):
                row = (start // LANES * planes + q) * rows + i
                staged[pl.ds(row, blocks, stride=pitch), :] = block[q * blocks : (q + 1) * blocks, :]
    for b in range(blocks):
        sent_ref[height * b : height * (b + 1), :] = staged[pitch * b : pitch * b + height, :]
    keep_east.wait()
    keep_north.wait()


def gather_in(
    a_ref, b_ref, control_hbm, east_hbm, north_hbm, out_hbm,
    control, east, north, field, turned, flat, staged, sems,
):
    planes, lon, lat = control.shape
    rows, steps = field.shape[:2]
    blocks = lat // rows
    pitch = staged.shape[0] // blocks
    fetches = [
        pltpu.make_async_copy(source, target, sems.at[planes + n])
        for n, (source, target) in enumerate(
            ((east_hbm, east), (north_hbm, north), (control_hbm, control))
        )
    ]
    for fetch in fetches:
        fetch.start()
    at = 0
    for in_ref in (a_ref, b_ref):
        height = in_ref.shape[0] // blocks
        for b in range(blocks):
            staged[pitch * b + at : pitch * b + at + height, :] = in_ref[
                height * b : height * (b + 1), :
            ]
        at += height
    for i in range(rows):
        for start, width in blocks_of(lon):
            picked = [
                staged[pl.ds((start // LANES * planes + q) * rows + i, blocks, stride=pitch), :]
                for q in range(planes)
            ]
            flat[i, start : start + LANES, :] = jnp.concatenate(picked, 0).T
        for r in range(steps):
            field[i, r] = flat[i, pl.ds(r, SUB, stride=steps), :]
    fetches[0].wait()
    fetches[1].wait()
    diffuse_in_place(field, east, north)
    for i in range(rows):
        for r in range(steps):
            flat[i, pl.ds(r, SUB, stride=steps), :] = field[i, r]
        for start, width in blocks_of(lon):
            block = flat[i, start : start + LANES, :].T
            for q in range(planes):
                turned[start // LANES, pl.ds(lat * q + i, blocks, stride=rows), :] = block[
                    q * blocks : (q + 1) * blocks, :
                ]
    fetches[2].wait()
    stores = []
    for q in range(planes):
        for start, width in blocks_of(lon):
            back = turned[start // LANES, lat * q : lat * q + lat, :].T
            place = pl.ds(start, width)
            control[q, place, :] = control[q, place, :] + back[:width, :]
        stores.append(pltpu.make_async_copy(control.at[q], out_hbm.at[q], sems.at[q]))
        stores[-1].start()
    for store in stores:
        store.wait()


def prepare(core_ref, filter_ref, table_ref, count_ref, kind_ref, band_ref, band_t_ref, *weight_refs):
    levels = filter_ref.shape[0]
    flat = band_ref.shape[0]
    rows = flat // levels
    kinds, columns = table_ref.shape
    lon = count_ref.shape[1]
    own = weight_refs[0].shape[0]
    variables = columns // levels
    share = own // variables // rows
    spread = ones_where(iota((flat, levels), 0) // rows == iota((flat, levels), 1))
    spread_t = ones_where(iota((levels, flat), 1) // rows == iota((levels, flat), 0))
    same = lax.rem(iota((flat, flat), 0), rows) == lax.rem(iota((flat, flat), 1), rows)
    weight = filter_ref[...]
    band_ref[...] = jnp.where(same, dot(dot(spread, weight), spread_t), 0.0)
    band_t_ref[...] = jnp.where(same, dot(dot(spread, weight, ((1,), (1,))), spread_t), 0.0)
    row = iota((own, columns), 0)
    column = (
        row // (share * rows) * levels
        + core_ref[0] * share
        + lax.rem(row // rows, share)
    )
    picked = dot(ones_where(column == iota((own, columns), 1)), table_ref[...], ((1,), (1,)))
    wide = kinds * rows
    each = ones_where(iota((kinds, wide), 1) // rows == iota((kinds, wide), 0))
    match = lax.rem(iota((own, wide), 0), rows) == lax.rem(iota((own, wide), 1), rows)
    table = jnp.where(match, dot(picked, each), 0.0)
    repeat = ones_where(lax.rem(iota((wide, rows), 0), rows) == iota((wide, rows), 1))
    kind = dot(repeat, kind_ref[...].astype(jnp.float32))
    count = dot(repeat, count_ref[...].astype(jnp.float32))
    which = (iota((wide, lon), 0) // rows).astype(jnp.float32)
    chosen = jnp.where(kind == which, count, 0.0)
    start = 0
    for weight_ref in weight_refs[:-1]:
        width = weight_ref.shape[1]
        weight_ref[...] = dot(table, chosen[:, start : start + width])
        start += width
    tail = jnp.concatenate(
        [chosen[:, start:], jnp.zeros((wide, start + LANES - lon), jnp.float32)], 1
    )
    weight_refs[-1][...] = dot(table, tail).T[: lon - start, :]


def rows_of(perturb_ref, out_ref):
    levels, rows, lon = perturb_ref.shape
    pair = SUB // rows
    for tile, (start, width) in enumerate(blocks_of(lon)):
        if width < LANES:
            out_ref[tile] = jnp.zeros(out_ref.shape[1:], jnp.float32)
        for t in range(levels // pair):
            out_ref[tile, SUB * t : SUB * t + SUB, :width] = jnp.concatenate(
                [perturb_ref[pair * t + u, :, start : start + width] for u in range(pair)], 0
            )


def fetch_tiles(first, perturb_hbm, perturb, sems):
    copies = [
        pltpu.make_async_copy(perturb_hbm.at[first + u], perturb.at[u], sems.at[u])
        for u in range(perturb.shape[0])
    ]
    for copy in copies:
        copy.start()
    return copies


def partial_sums(
    first, core_ref, band_ref, pieces_ref, perturb_hbm, send_ref, keep_ref,
    perturb, filtered, parts, sems,
):
    count, products, flat = perturb.shape[:3]
    members = filtered.shape[1] // LANES
    variables = products // members
    piece = pieces_ref.shape[2] // members
    core = core_ref[0]
    half = flat // 2
    copies = fetch_tiles(first, perturb_hbm, perturb, sems)
    for u in range(count):
        mine = [
            pieces_ref[:, first + u, piece * k : piece * k + piece, :].reshape(flat, LANES)
            for k in range(members)
        ]
        filtered[...] = dot(band_ref[...], jnp.concatenate(mine, 1))
        copies[u].wait()
        for side, out_ref in enumerate((send_ref, keep_ref)):
            base = (core if side else 1 - core) * half
            turned = out_ref.shape[0] < variables * half
            to_ref = parts.at[side] if turned else out_ref
            for t in range(half // SUB):
                at = pl.ds(pl.multiple_of(base + t * SUB, SUB), SUB)
                fields = [filtered[at, LANES * k : LANES * (k + 1)] for k in range(members)]
                for v in range(variables):
                    total = perturb[u, v, at, :] * fields[0]
                    for k in range(1, members):
                        total = total + perturb[u, k * variables + v, at, :] * fields[k]
                    row = v * half + t * SUB
                    to_ref[row : row + SUB, u * LANES : (u + 1) * LANES] = total
            if turned:
                for v in range(variables):
                    block = parts[side, v * half : (v + 1) * half, :].T
                    out_ref[:, v * half : (v + 1) * half] = block[: out_ref.shape[0], :]


def lift(first, place, core_ref, band_ref, own_ref, other_ref, perturb_hbm, *rest):
    out_ref, perturb, adjoint, parts, sems = rest[-5:]
    count, products, flat = perturb.shape[:3]
    members = adjoint.shape[1] // LANES
    variables = products // members
    piece = out_ref.shape[2] // members
    core = core_ref[0]
    half = flat // 2
    copies = fetch_tiles(first, perturb_hbm, perturb, sems)
    for earlier_ref in rest[:-5]:
        out_ref[:, :place] = earlier_ref[...]
    sides = [own_ref, other_ref]
    if own_ref.shape[0] < variables * half:
        empty = jnp.zeros((LANES - own_ref.shape[0], half), jnp.float32)
        for side, weighted in enumerate(sides):
            for v in range(variables):
                block = jnp.concatenate([weighted[:, v * half : (v + 1) * half], empty], 0)
                parts[side, v * half : (v + 1) * half, :] = block.T
        sides = [parts.at[0], parts.at[1]]
    for u in range(count):
        copies[u].wait()
        for side, weighted in enumerate(sides):
            base = (core if side == 0 else 1 - core) * half
            for t in range(half // SUB):
                at = pl.ds(pl.multiple_of(base + t * SUB, SUB), SUB)
                terms = []
                for v in range(variables):
                    row = v * half + t * SUB
                    terms.append(weighted[row : row + SUB, u * LANES : (u + 1) * LANES])
                for k in range(members):
                    total = perturb[u, k * variables, at, :] * terms[0]
                    for v in range(1, variables):
                        total = total + perturb[u, k * variables + v, at, :] * terms[v]
                    adjoint[at, LANES * k : LANES * (k + 1)] = total
        whole = dot(band_ref[...], adjoint[...])
        for k in range(members):
            out_ref[:, place + u, piece * k : piece * k + piece, :] = whole[
                :, LANES * k : LANES * (k + 1)
            ].reshape(-1, piece, LANES)


def add_up(keep_ref, got_ref, out_ref):
    out_ref[...] = keep_ref[...] + got_ref[...]


def weigh(weight_ref, on_chip_ref, got_ref, out_ref):
    out_ref[...] = weight_ref[...] * (on_chip_ref[...] + got_ref[...])


def call(kernel, out_shape, flops, moved, ins=None, outs=None, scratch=(), limit=8, **grid):
    def run(*args):
        return pl.pallas_call(
            kernel,
            out_shape=out_shape,
            in_specs=ins or [VMEM] * len(args),
            out_specs=outs or jax.tree.map(lambda _: VMEM, out_shape),
            scratch_shapes=scratch,
            cost_estimate=pl.CostEstimate(flops=flops, bytes_accessed=moved, transcendentals=0),
            compiler_params=pltpu.CompilerParams(vmem_limit_bytes=limit << 20),
            **grid,
        )(*args)

    return run


def f32(*shape):
    return jax.ShapeDtypeStruct(shape, jnp.float32)


def local(control, perturb, obs_count, obs_kind, obs_table, band_filter, diffusivity):
    members, level_planes, lat, lon = control.shape
    variables, levels, rows = perturb.shape[1:4]
    devices = lax.axis_size("wide")
    planes = members * level_planes
    steps = lon // SUB
    flat = levels * rows
    half = flat // 2
    tiles = -(-lon // LANES)
    chunks = [(0, 2), (2, tiles - 3), (tiles - 1, 1)]
    groups = [(0, 2), (2, tiles - 2), (2, tiles - 2)]
    height = planes * rows
    control_t = jnp.swapaxes(control, 2, 3).reshape(planes, lon, lat)
    control_t = pltpu.with_memory_space_constraint(control_t, pltpu.HBM)
    diff_t = jnp.swapaxes(diffusivity, 0, 1)
    core = (lax.axis_index("mem") % 2).astype(jnp.int32).reshape(1)

    coefs = f32(rows, steps, SUB, LANES)
    vmem = [
        (planes, lon, lat),
        coefs.shape,
        coefs.shape,
        coefs.shape,
        (tiles, planes * lat, LANES),
        (rows, tiles * LANES, LANES),
        (devices * (tiles * height + rows), LANES),
    ]
    vmem = [pltpu.VMEM(shape, jnp.float32) for shape in vmem]
    resting = pltpu.HBM(coefs.shape, jnp.float32)
    work = planes * lat * lon * ITERS * 8
    size = planes * lat * lon * 4

    sent, east, north = call(
        spread_out,
        [f32(devices * tiles * height, LANES), resting, resting],
        work,
        2 * size,
        [HBM, HBM],
        [VMEM, HBM, HBM],
        [pltpu.VMEM((lon, lat), jnp.float32), *vmem, pltpu.SemaphoreType.DMA((4,))],
        20,
    )(control_t, pltpu.with_memory_space_constraint(diff_t, pltpu.HBM))
    east, north = (pltpu.with_memory_space_constraint(e, pltpu.HBM) for e in (east, north))

    def exchange(sent):
        return lax.all_to_all(sent.reshape(devices, -1, height, LANES), "wide", 0, 0, tiled=True)

    pieces = exchange(sent)

    used = lon - (tiles - 1) * LANES
    parts = [f32(variables * half, count * LANES) for first, count in chunks[:-1]]
    parts.append(f32(used, variables * half))
    band, band_t, *weights = call(
        prepare,
        [f32(flat, flat), f32(flat, flat)] + parts,
        1 << 28,
        4 << 20,
        [SMEM] + [VMEM] * 4,
    )(core, band_filter, obs_table, obs_count, obs_kind)
    perturb = perturb.reshape(members * variables, levels, rows, lon)
    perturb = call(
        rows_of,
        f32(tiles, members * variables, flat, LANES),
        1 << 20,
        6 * size,
        [pl.BlockSpec((None, levels, rows, lon), lambda g: (g, 0, 0, 0))],
        pl.BlockSpec((tiles, None, flat, LANES), lambda g: (0, g, 0, 0)),
        grid=(members * variables,),
    )(pltpu.with_memory_space_constraint(perturb, pltpu.HBM))
    perturb = pltpu.with_memory_space_constraint(perturb, pltpu.HBM)

    other_core = [(i, i ^ 1) for i in range(4)]
    next_chip = [(i, i ^ 2) for i in range(4)]
    home = None
    lifted = []
    for h, (first, count) in enumerate(chunks):
        part = parts[h]
        scratch = [
            pltpu.VMEM((count, members * variables, flat, LANES), jnp.float32),
            pltpu.VMEM((flat, members * LANES), jnp.float32),
            pltpu.VMEM((2, variables * half, LANES), jnp.float32),
            pltpu.SemaphoreType.DMA((count,)),
        ]
        send, keep = call(
            functools.partial(partial_sums, first),
            [part, part],
            count << 28,
            count * size,
            [SMEM, VMEM, VMEM, HBM],
            None,
            scratch,
        )(core, band, pieces, perturb)
        got = lax.ppermute(send, "mem", other_core)
        on_chip = call(add_up, part, 1 << 18, size)(keep, got)
        got = lax.ppermute(on_chip, "mem", next_chip)
        own = call(weigh, part, 1 << 18, size)(weights[h], on_chip, got)
        other = lax.ppermute(own, "mem", other_core)
        start, total = groups[h]
        place = first - start
        begins = place == 0

        home = call(
            functools.partial(lift, first, place),
            f32(devices, place + count, height, LANES),
            count << 28,
            count * size,
            [SMEM, VMEM, VMEM, VMEM, HBM] + ([] if begins else [VMEM]),
            None,
            scratch,
        )(core, band_t, own, other, perturb, *([] if begins else [home]))
        if first + count == start + total:
            lifted.append(exchange(home).reshape(-1, LANES))

    out = call(
        gather_in,
        pltpu.HBM((planes, lon, lat), jnp.float32),
        work,
        3 * size,
        [VMEM, VMEM, HBM, HBM, HBM],
        HBM,
        [*vmem, pltpu.SemaphoreType.DMA((planes + 3,))],
        20,
    )(*lifted, control_t, east, north)
    return jnp.swapaxes(out.reshape(members, level_planes, lon, lat), 2, 3)


def solution(mesh):
    placed = (
        P("mem", "wide", None, None),
        P("mem", None, None, "wide", None),
        P("wide", None),
        P("wide", None),
        P(),
        P(),
        P(),
    )

    return jax.shard_map(
        local, mesh=mesh, in_specs=placed, out_specs=P("mem", "wide", None, None), check_vma=False
    )
```

```python
import functools

import jax
import jax.numpy as jnp
from jax import lax
from jax.experimental import pallas as pl
from jax.experimental.pallas import tpu as pltpu
from jax.sharding import PartitionSpec as P


ITERS = 16
UNROLL = 8
SUB = 8
LANES = 128
VMEM = pl.BlockSpec(memory_space=pltpu.VMEM)
SMEM = pl.BlockSpec(memory_space=pltpu.SMEM)
HBM = pl.BlockSpec(memory_space=pltpu.HBM)
HIGHEST = lax.Precision.HIGHEST


def dot(a, b, contract=((1,), (0,))):
    return lax.dot_general(
        a, b, (contract, ((), ())), precision=HIGHEST, preferred_element_type=jnp.float32
    )


def iota(shape, dim):
    return lax.broadcasted_iota(jnp.int32, shape, dim)


def ones_where(mask):
    return jnp.where(mask, 1.0, 0.0).astype(jnp.float32)


def blocks_of(lon):
    return [(start, min(LANES, lon - start)) for start in range(0, lon, LANES)]


def coefficients(diff_ref, east, north, turned, flat):
    rows, steps = east.shape[:2]
    lon, lat = diff_ref.shape
    blocks = lat // rows
    copies = LANES // blocks
    for start, width in blocks_of(lon):
        turned[start // LANES, :lat, :width] = diff_ref[start : start + width, :].T
    for i in range(rows):
        for start, width in blocks_of(lon):
            picked = turned[start // LANES, pl.ds(i, blocks, stride=rows), :]
            flat[i, start : start + LANES, :] = jnp.concatenate([picked] * copies, 0).T
    edge = lax.rem(iota((SUB, LANES), 1), blocks) == blocks - 1
    first = [flat[i, pl.ds(0, SUB, stride=steps), :] for i in range(rows)]
    here = list(first)
    for r in range(steps):
        for i in range(rows):
            if r + 1 < steps:
                there = flat[i, pl.ds(r + 1, SUB, stride=steps), :]
            else:
                there = pltpu.roll(first[i], SUB - 1, 0)
            east[i, r] = 0.5 * (here[i] + there)
            if i + 1 < rows:
                north[i, r] = 0.5 * (here[i] + here[i + 1])
            else:
                up = 0.5 * (here[i] + pltpu.roll(start_of_row, LANES - 1, 1))
                north[i, r] = jnp.where(edge, jnp.zeros_like(up), up)
            if i == 0:
                start_of_row = here[0]
            here[i] = there if i else here[i]
            if i == 0:
                next_of_row = there
        here[0] = next_of_row


def diffuse_in_place(field, east, north):
    rows, steps = field.shape[:2]

    def one_step(step_index, carry):
        here = [field[i, 0] for i in range(rows)]
        ahead = [pltpu.roll(f, SUB - 1, 0) for f in here]
        before = [
            pltpu.roll(east[i, steps - 1] * (ahead[i] - field[i, steps - 1]), 1, 0)
            for i in range(rows)
        ]
        for r in range(steps):
            there = [field[i, r + 1] if r + 1 < steps else ahead[i] for i in range(rows)]
            up = here[1:] + [pltpu.roll(here[0], LANES - 1, 1)]
            flux_north = [north[i, r] * (up[i] - here[i]) for i in range(rows)]
            down = [pltpu.roll(flux_north[-1], 1, 1)] + flux_north[:-1]
            for i in range(rows):
                flux_east = east[i, r] * (there[i] - here[i])
                field[i, r] = here[i] + ((flux_east - before[i]) + (flux_north[i] - down[i]))
                before[i] = flux_east
            here = there
        return carry

    lax.fori_loop(0, ITERS, one_step, 0, unroll=UNROLL)


def spread_out(
    control_hbm, diff_hbm, sent_hbm, east_hbm, north_hbm,
    diffusivity, ready, control, east, north, field, turned, flat, staged, sems,
):
    planes, lon, lat = control.shape
    rows, steps = field.shape[:2]
    blocks = lat // rows
    tiles = turned.shape[0]
    height = planes * rows
    pitch = staged.shape[0] // blocks
    fetch_diff = pltpu.make_async_copy(diff_hbm, diffusivity, sems.at[0])
    fetch_diff.start()
    fetch = pltpu.make_async_copy(control_hbm, control, sems.at[1])
    fetch.start()
    turned[tiles - 1] = jnp.zeros(turned.shape[1:], jnp.float32)
    flat[:, (tiles - 1) * LANES :, :] = jnp.zeros((rows, LANES, LANES), jnp.float32)
    fetch_diff.wait()
    coefficients(diffusivity, east, north, turned, flat)
    keep_east = pltpu.make_async_copy(east, east_hbm, sems.at[2])
    keep_north = pltpu.make_async_copy(north, north_hbm, sems.at[3])
    keep_east.start()
    keep_north.start()
    fetch.wait()
    for q in range(planes):
        for start, width in blocks_of(lon):
            turned[start // LANES, lat * q : lat * q + lat, :width] = control[
                q, start : start + width, :
            ].T
    for i in range(rows):
        for start, width in blocks_of(lon):
            picked = [
                turned[start // LANES, pl.ds(lat * q + i, blocks, stride=rows), :]
                for q in range(planes)
            ]
            flat[i, start : start + LANES, :] = jnp.concatenate(picked, 0).T
        for r in range(steps):
            field[i, r] = flat[i, pl.ds(r, SUB, stride=steps), :]
    diffuse_in_place(field, east, north)
    for i in range(rows):
        for r in range(steps):
            flat[i, pl.ds(r, SUB, stride=steps), :] = field[i, r]
    stores = []
    for tile in range(tiles):
        for i in range(rows):
            block = flat[i, tile * LANES : (tile + 1) * LANES, :].T
            for q in range(planes):
                staged[pl.ds((tile * planes + q) * rows + i, blocks, stride=pitch), :] = block[
                    q * blocks : (q + 1) * blocks, :
                ]
        for b in range(blocks):
            start = pitch * b + height * tile
            ready[tile, b] = staged[start : start + height, :]
        stores.append(
            pltpu.make_async_copy(ready.at[tile], sent_hbm.at[:, tile], sems.at[4 + tile])
        )
        stores[-1].start()
    for store in stores:
        store.wait()
    keep_east.wait()
    keep_north.wait()


def gather_in(
    a_ref, b_ref, control_hbm, east_hbm, north_hbm, out_hbm,
    control, east, north, field, turned, flat, staged, sems,
):
    planes, lon, lat = control.shape
    rows, steps = field.shape[:2]
    blocks = lat // rows
    pitch = staged.shape[0] // blocks
    fetches = [
        pltpu.make_async_copy(source, target, sems.at[planes + n])
        for n, (source, target) in enumerate(
            ((east_hbm, east), (north_hbm, north), (control_hbm, control))
        )
    ]
    for fetch in fetches:
        fetch.start()
    at = 0
    for in_ref in (a_ref, b_ref):
        height = in_ref.shape[0] // blocks
        for b in range(blocks):
            staged[pitch * b + at : pitch * b + at + height, :] = in_ref[
                height * b : height * (b + 1), :
            ]
        at += height
    for i in range(rows):
        for start, width in blocks_of(lon):
            picked = [
                staged[pl.ds((start // LANES * planes + q) * rows + i, blocks, stride=pitch), :]
                for q in range(planes)
            ]
            flat[i, start : start + LANES, :] = jnp.concatenate(picked, 0).T
        for r in range(steps):
            field[i, r] = flat[i, pl.ds(r, SUB, stride=steps), :]
    fetches[0].wait()
    fetches[1].wait()
    diffuse_in_place(field, east, north)
    for i in range(rows):
        for r in range(steps):
            flat[i, pl.ds(r, SUB, stride=steps), :] = field[i, r]
        for start, width in blocks_of(lon):
            block = flat[i, start : start + LANES, :].T
            for q in range(planes):
                turned[start // LANES, pl.ds(lat * q + i, blocks, stride=rows), :] = block[
                    q * blocks : (q + 1) * blocks, :
                ]
    fetches[2].wait()
    stores = []
    for q in range(planes):
        for start, width in blocks_of(lon):
            back = turned[start // LANES, lat * q : lat * q + lat, :].T
            place = pl.ds(start, width)
            control[q, place, :] = control[q, place, :] + back[:width, :]
        stores.append(pltpu.make_async_copy(control.at[q], out_hbm.at[q], sems.at[q]))
        stores[-1].start()
    for store in stores:
        store.wait()


def prepare(core_ref, filter_ref, table_ref, count_ref, kind_ref, band_ref, band_t_ref, *weight_refs):
    levels = filter_ref.shape[0]
    flat = band_ref.shape[0]
    rows = flat // levels
    kinds, columns = table_ref.shape
    lon = count_ref.shape[1]
    own = weight_refs[0].shape[0]
    variables = columns // levels
    share = own // variables // rows
    spread = ones_where(iota((flat, levels), 0) // rows == iota((flat, levels), 1))
    spread_t = ones_where(iota((levels, flat), 1) // rows == iota((levels, flat), 0))
    same = lax.rem(iota((flat, flat), 0), rows) == lax.rem(iota((flat, flat), 1), rows)
    weight = filter_ref[...]
    band_ref[...] = jnp.where(same, dot(dot(spread, weight), spread_t), 0.0)
    band_t_ref[...] = jnp.where(same, dot(dot(spread, weight, ((1,), (1,))), spread_t), 0.0)
    row = iota((own, columns), 0)
    column = (
        row // (share * rows) * levels
        + core_ref[0] * share
        + lax.rem(row // rows, share)
    )
    picked = dot(ones_where(column == iota((own, columns), 1)), table_ref[...], ((1,), (1,)))
    wide = kinds * rows
    each = ones_where(iota((kinds, wide), 1) // rows == iota((kinds, wide), 0))
    match = lax.rem(iota((own, wide), 0), rows) == lax.rem(iota((own, wide), 1), rows)
    table = jnp.where(match, dot(picked, each), 0.0)
    repeat = ones_where(lax.rem(iota((wide, rows), 0), rows) == iota((wide, rows), 1))
    kind = dot(repeat, kind_ref[...].astype(jnp.float32))
    count = dot(repeat, count_ref[...].astype(jnp.float32))
    which = (iota((wide, lon), 0) // rows).astype(jnp.float32)
    chosen = jnp.where(kind == which, count, 0.0)
    start = 0
    for weight_ref in weight_refs[:-1]:
        width = weight_ref.shape[1]
        weight_ref[...] = dot(table, chosen[:, start : start + width])
        start += width
    tail = jnp.concatenate(
        [chosen[:, start:], jnp.zeros((wide, start + LANES - lon), jnp.float32)], 1
    )
    weight_refs[-1][...] = dot(table, tail).T[: lon - start, :]


def rows_of(perturb_ref, out_ref):
    levels, rows, lon = perturb_ref.shape
    pair = SUB // rows
    for tile, (start, width) in enumerate(blocks_of(lon)):
        if width < LANES:
            out_ref[tile] = jnp.zeros(out_ref.shape[1:], jnp.float32)
        for t in range(levels // pair):
            out_ref[tile, SUB * t : SUB * t + SUB, :width] = jnp.concatenate(
                [perturb_ref[pair * t + u, :, start : start + width] for u in range(pair)], 0
            )


def fetch_tiles(first, perturb_hbm, perturb, sems):
    copies = [
        pltpu.make_async_copy(perturb_hbm.at[first + u], perturb.at[u], sems.at[u])
        for u in range(perturb.shape[0])
    ]
    for copy in copies:
        copy.start()
    return copies


def partial_sums(
    first, core_ref, band_ref, pieces_ref, perturb_hbm, send_ref, keep_ref,
    perturb, filtered, parts, sems,
):
    count, products, flat = perturb.shape[:3]
    members = filtered.shape[1] // LANES
    variables = products // members
    piece = pieces_ref.shape[2] // members
    core = core_ref[0]
    half = flat // 2
    copies = fetch_tiles(first, perturb_hbm, perturb, sems)
    for u in range(count):
        mine = [
            pieces_ref[:, first + u, piece * k : piece * k + piece, :].reshape(flat, LANES)
            for k in range(members)
        ]
        filtered[...] = dot(band_ref[...], jnp.concatenate(mine, 1))
        copies[u].wait()
        for side, out_ref in enumerate((send_ref, keep_ref)):
            base = (core if side else 1 - core) * half
            turned = out_ref.shape[0] < variables * half
            to_ref = parts.at[side] if turned else out_ref
            for t in range(half // SUB):
                at = pl.ds(pl.multiple_of(base + t * SUB, SUB), SUB)
                fields = [filtered[at, LANES * k : LANES * (k + 1)] for k in range(members)]
                for v in range(variables):
                    total = perturb[u, v, at, :] * fields[0]
                    for k in range(1, members):
                        total = total + perturb[u, k * variables + v, at, :] * fields[k]
                    row = v * half + t * SUB
                    to_ref[row : row + SUB, u * LANES : (u + 1) * LANES] = total
            if turned:
                for v in range(variables):
                    block = parts[side, v * half : (v + 1) * half, :].T
                    out_ref[:, v * half : (v + 1) * half] = block[: out_ref.shape[0], :]


def lift(
    first, place, fetched, ahead, core_ref, band_ref, own_ref, other_ref, perturb_ref, *rest
):
    *rest, adjoint, parts, sems = rest
    perturb = perturb_ref if fetched else rest.pop()
    count, products, flat = perturb.shape[:3]
    copies = [] if fetched else fetch_tiles(first, perturb_ref, perturb, sems)
    if ahead:
        tail = pltpu.make_async_copy(perturb_ref.at[first + count], rest.pop().at[0], sems.at[count])
        tail.start()
    *earlier, out_ref = rest
    members = adjoint.shape[1] // LANES
    variables = products // members
    piece = out_ref.shape[2] // members
    core = core_ref[0]
    half = flat // 2
    for earlier_ref in earlier:
        out_ref[:, :place] = earlier_ref[...]
    sides = [own_ref, other_ref]
    if own_ref.shape[0] < variables * half:
        empty = jnp.zeros((LANES - own_ref.shape[0], half), jnp.float32)
        for side, weighted in enumerate(sides):
            for v in range(variables):
                block = jnp.concatenate([weighted[:, v * half : (v + 1) * half], empty], 0)
                parts[side, v * half : (v + 1) * half, :] = block.T
        sides = [parts.at[0], parts.at[1]]
    for u in range(count):
        if copies:
            copies[u].wait()
        for side, weighted in enumerate(sides):
            base = (core if side == 0 else 1 - core) * half
            for t in range(half // SUB):
                at = pl.ds(pl.multiple_of(base + t * SUB, SUB), SUB)
                terms = []
                for v in range(variables):
                    row = v * half + t * SUB
                    terms.append(weighted[row : row + SUB, u * LANES : (u + 1) * LANES])
                for k in range(members):
                    total = perturb[u, k * variables, at, :] * terms[0]
                    for v in range(1, variables):
                        total = total + perturb[u, k * variables + v, at, :] * terms[v]
                    adjoint[at, LANES * k : LANES * (k + 1)] = total
        whole = dot(band_ref[...], adjoint[...])
        for k in range(members):
            out_ref[:, place + u, piece * k : piece * k + piece, :] = whole[
                :, LANES * k : LANES * (k + 1)
            ].reshape(-1, piece, LANES)
    if ahead:
        tail.wait()


def add_up(keep_ref, got_ref, out_ref):
    out_ref[...] = keep_ref[...] + got_ref[...]


def weigh(weight_ref, on_chip_ref, got_ref, out_ref):
    out_ref[...] = weight_ref[...] * (on_chip_ref[...] + got_ref[...])


def call(kernel, out_shape, flops, moved, ins=None, outs=None, scratch=(), limit=8, **grid):
    def run(*args):
        return pl.pallas_call(
            kernel,
            out_shape=out_shape,
            in_specs=ins or [VMEM] * len(args),
            out_specs=outs or jax.tree.map(lambda _: VMEM, out_shape),
            scratch_shapes=scratch,
            cost_estimate=pl.CostEstimate(flops=flops, bytes_accessed=moved, transcendentals=0),
            compiler_params=pltpu.CompilerParams(vmem_limit_bytes=limit << 20),
            **grid,
        )(*args)

    return run


def f32(*shape):
    return jax.ShapeDtypeStruct(shape, jnp.float32)


def local(control, perturb, obs_count, obs_kind, obs_table, band_filter, diffusivity):
    members, level_planes, lat, lon = control.shape
    variables, levels, rows = perturb.shape[1:4]
    devices = lax.axis_size("wide")
    planes = members * level_planes
    steps = lon // SUB
    flat = levels * rows
    half = flat // 2
    tiles = -(-lon // LANES)
    chunks = [(0, 2), (2, tiles - 3), (tiles - 1, 1)]
    groups = [(0, 2), (2, tiles - 2), (2, tiles - 2)]
    height = planes * rows
    control_t = jnp.swapaxes(control, 2, 3).reshape(planes, lon, lat)
    control_t = pltpu.with_memory_space_constraint(control_t, pltpu.HBM)
    diff_t = jnp.swapaxes(diffusivity, 0, 1)
    core = (lax.axis_index("mem") % 2).astype(jnp.int32).reshape(1)

    coefs = f32(rows, steps, SUB, LANES)
    vmem = [
        (planes, lon, lat),
        coefs.shape,
        coefs.shape,
        coefs.shape,
        (tiles, planes * lat, LANES),
        (rows, tiles * LANES, LANES),
        (devices * (tiles * height + rows), LANES),
    ]
    vmem = [pltpu.VMEM(shape, jnp.float32) for shape in vmem]
    resting = pltpu.HBM(coefs.shape, jnp.float32)
    work = planes * lat * lon * ITERS * 8
    size = planes * lat * lon * 4

    sent, east, north = call(
        spread_out,
        [pltpu.HBM((devices, tiles, height, LANES), jnp.float32), resting, resting],
        work,
        2 * size,
        [HBM, HBM],
        [HBM] * 3,
        [
            pltpu.VMEM((lon, lat), jnp.float32),
            pltpu.VMEM((tiles, devices, height, LANES), jnp.float32),
            *vmem,
            pltpu.SemaphoreType.DMA((4 + tiles,)),
        ],
        20,
    )(control_t, pltpu.with_memory_space_constraint(diff_t, pltpu.HBM))
    east, north = (pltpu.with_memory_space_constraint(e, pltpu.HBM) for e in (east, north))

    def exchange(sent):
        return lax.all_to_all(sent.reshape(devices, -1, height, LANES), "wide", 0, 0, tiled=True)

    pieces = exchange(sent)

    used = lon - (tiles - 1) * LANES
    parts = [f32(variables * half, count * LANES) for first, count in chunks[:-1]]
    parts.append(f32(used, variables * half))
    band, band_t, *weights = call(
        prepare,
        [f32(flat, flat), f32(flat, flat)] + parts,
        1 << 28,
        4 << 20,
        [SMEM] + [VMEM] * 4,
    )(core, band_filter, obs_table, obs_count, obs_kind)
    perturb = perturb.reshape(members * variables, levels, rows, lon)
    perturb = call(
        rows_of,
        f32(tiles, members * variables, flat, LANES),
        1 << 20,
        6 * size,
        [pl.BlockSpec((None, levels, rows, lon), lambda g: (g, 0, 0, 0))],
        pl.BlockSpec((tiles, None, flat, LANES), lambda g: (0, g, 0, 0)),
        grid=(members * variables,),
    )(pltpu.with_memory_space_constraint(perturb, pltpu.HBM))
    perturb = pltpu.with_memory_space_constraint(perturb, pltpu.HBM)

    other_core = [(i, i ^ 1) for i in range(4)]
    next_chip = [(i, i ^ 2) for i in range(4)]
    home = None
    lifted = []
    for h, (first, count) in enumerate(chunks):
        part = parts[h]
        room = (count, members * variables, flat, LANES)
        scratch = [
            pltpu.VMEM(room, jnp.float32),
            pltpu.VMEM((flat, members * LANES), jnp.float32),
            pltpu.VMEM((2, variables * half, LANES), jnp.float32),
            pltpu.SemaphoreType.DMA((count + 1,)),
        ]
        keeps = h == 0
        send, keep, *tiles_here = call(
            functools.partial(partial_sums, first),
            [part, part] + ([pltpu.VMEM(room, jnp.float32)] if keeps else []),
            count << 28,
            count * size,
            [SMEM, VMEM, VMEM, HBM],
            None,
            scratch[1:] if keeps else scratch,
        )(core, band, pieces, perturb)
        got = lax.ppermute(send, "mem", other_core)
        on_chip = call(add_up, part, 1 << 18, size)(keep, got)
        got = lax.ppermute(on_chip, "mem", next_chip)
        own = call(weigh, part, 1 << 18, size)(weights[h], on_chip, got)
        other = lax.ppermute(own, "mem", other_core)
        start, total = groups[h]
        place = first - start
        begins = place == 0

        fetched, ahead = h != 1, h == 1
        rows_here = tiles_here[0] if keeps else tail if fetched else perturb
        tile_room = pltpu.VMEM((1, *room[1:]), jnp.float32)
        home, *tails = call(
            functools.partial(lift, first, place, fetched, ahead),
            [f32(devices, place + count, height, LANES)] + ([tile_room] if ahead else []),
            count << 28,
            count * size,
            [SMEM, VMEM, VMEM, VMEM, VMEM if fetched else HBM] + ([] if begins else [VMEM]),
            None,
            scratch[1:] if fetched else scratch,
        )(core, band_t, own, other, rows_here, *([] if begins else [home]))
        tail = tails[0] if tails else None
        if first + count == start + total:
            lifted.append(exchange(home).reshape(-1, LANES))

    out = call(
        gather_in,
        pltpu.HBM((planes, lon, lat), jnp.float32),
        work,
        3 * size,
        [VMEM, VMEM, HBM, HBM, HBM],
        HBM,
        [*vmem, pltpu.SemaphoreType.DMA((planes + 3,))],
        20,
    )(*lifted, control_t, east, north)
    return jnp.swapaxes(out.reshape(members, level_planes, lon, lat), 2, 3)


def solution(mesh):
    placed = (
        P("mem", "wide", None, None),
        P("mem", None, None, "wide", None),
        P("wide", None),
        P("wide", None),
        P(),
        P(),
        P(),
    )

    return jax.shard_map(
        local, mesh=mesh, in_specs=placed, out_specs=P("mem", "wide", None, None), check_vma=False
    )
```
